512 devices in a mesh: grp: 16 (over z_lo, y), band: 32 (over z_hi, x, core).
Axes of the slice: x: 4, y: 4, z: 16 (z_hi: 4, z_lo: 4; z = z_hi * 4 + z_lo), core: 2. Of those that a mesh axis runs over, the one named last changes fastest.
Arguments:
- raw: bfloat16 [2, 256, 262144], P(None, 'band', 'grp'), may hold values from -6 to 6
- taps: int32 [5, 2, 4, 512], replicated, may hold values from 0 to 255, as said below
- weights: float32 [5, 2, 4, 512], replicated, may hold values from -0.11 to 1.6, as said below
- shifts: float32 [5], replicated, may hold values from 1 to 3
Outputs:
- image: bfloat16 [2, 262144, 256], P(None, ('grp', 'band'))
The draws below stay inside these ranges and needn't reach their ends.
Inputs may be any that keep to these rules, and one draw needn't show every extreme that they name: taps[l, h, s, j] = c - 1 + s clipped to the half sector, where c is j / 2 or (j + 1) / 2 rounded down, clipped likewise. `weights`: each group of four coefficients is a cubic Lagrange stencil times a positive factor.
All inputs are finite; a program needn't handle non-finite values.
Results may differ from the reference program's by a relative error of at most 0.011.
Values may be sent and summed in bfloat16 or wider, within the bound.
A program may use at most 64 MiB of HBM per device.

```python
import math
import jax
import jax.numpy as jnp
import numpy as np
from jax import lax

NF = 256
ANGLES = 512
PULSE_DEV = 512
BAND_LEVELS = 3
LEVELS = 5
PULSES = 262144
N_GRP = 16
N_BAND = 32


def draw_taps(key, part):
    half_len = ANGLES // 2
    nudge = jax.random.randint(jax.random.fold_in(key, 11), (LEVELS, 2, 1, ANGLES), 0, 2)
    centre = jnp.clip((jnp.arange(ANGLES, dtype=jnp.int32)[None, None, None, :] + nudge) // 2, 0, half_len - 1)
    offsets = jnp.arange(4, dtype=jnp.int32)[None, None, :, None] - 1
    return jnp.clip(centre + offsets, 0, half_len - 1).astype(jnp.int32)


def draw_weights(key, part):
    fraction = jax.random.uniform(jax.random.fold_in(key, 21), (LEVELS, 2, 1, ANGLES), dtype=jnp.float32)
    row_gain = jnp.exp(jax.random.uniform(jax.random.fold_in(key, 22), (LEVELS, 2, 1, ANGLES), dtype=jnp.float32, minval=math.log(0.6), maxval=math.log(1.6)))
    tap_first = -fraction * (fraction - 1.0) * (fraction - 2.0) / 6.0
    tap_second = (fraction + 1.0) * (fraction - 1.0) * (fraction - 2.0) / 2.0
    tap_third = -(fraction + 1.0) * fraction * (fraction - 2.0) / 2.0
    tap_fourth = (fraction + 1.0) * fraction * (fraction - 1.0) / 6.0
    stencil = jnp.concatenate([tap_first, tap_second, tap_third, tap_fourth], axis=2)
    return (stencil * row_gain).astype(jnp.float32)


def block_levels(stream_key, dims, pieces, least, high):
    loudness = 1.0
    for position, parts in pieces:
        draws = jax.random.uniform(jax.random.fold_in(jax.random.fold_in(stream_key, 6), position), (parts,), jnp.float32, least / len(pieces), high / len(pieces))
        loudness = loudness * jnp.repeat(jnp.exp(draws), dims[position] // parts).reshape((-1,) + (1,) * (len(dims) - 1 - position))
    return loudness


def scatter_about(key, extent, width, most, cuts=(), kind=jnp.bfloat16):
    drawn = width * jax.random.normal(key, extent, jnp.float32)
    if cuts:
        drawn = drawn * block_levels(key, extent, cuts, -0.22, 0.18)
    return jnp.clip(drawn, -most, most).astype(kind)


def setup_inputs(seed: int = 0) -> dict:
    streams_of = jax.random.split(jax.random.key(seed), 5)
    return {
        "raw": scatter_about(streams_of[0], (2, NF, PULSES), 1.0, 6.0, ((1, 32), (2, 16))),
        "taps": draw_taps(jax.random.fold_in(streams_of[4], 71), 0),
        "weights": draw_weights(jax.random.fold_in(streams_of[4], 71), 0),
        "shifts": jnp.clip(jax.random.uniform(streams_of[3], (LEVELS,), jnp.float32, 1.0, 3.0), 1.0, 3.0),
    }


inv_root_two = 0.7071067811865476

def range_table(freq_count):
    column = jnp.arange(freq_count, dtype=jnp.int32)
    phases = (column[:, None] * column[None, :] % freq_count).astype(jnp.float32) * (2.0 * math.pi / freq_count)
    cosine = jnp.cos(phases)
    sine_map = jnp.sin(phases)
    real_rows = jnp.stack([cosine, -sine_map], axis=1)
    imag_rows = jnp.stack([sine_map, cosine], axis=1)
    return jnp.stack([real_rows, imag_rows], axis=0).astype(jnp.bfloat16)

def beam_table(angles, pulses):
    angle_ids = jnp.arange(angles, dtype=jnp.int32)
    pulse_ids = jnp.arange(pulses, dtype=jnp.int32)
    phases = (angle_ids[:, None] * pulse_ids[None, :] % angles).astype(jnp.float32) * (2.0 * math.pi / angles)
    cosine = jnp.cos(phases)
    sine_map = jnp.sin(phases)
    real_rows = jnp.stack([cosine, sine_map], axis=1)
    imag_rows = jnp.stack([-sine_map, cosine], axis=1)
    return jnp.stack([real_rows, imag_rows], axis=0).astype(jnp.bfloat16)

def interp_matrix(tap_rows, weight_rows, half_len):
    onehot = tap_rows[:, :, None] == jnp.arange(half_len, dtype=jnp.int32)[None, None, :]
    matrix = lax.optimization_barrier(jnp.sum(jnp.where(onehot, weight_rows[:, :, None], jnp.zeros((), weight_rows.dtype)), axis=0))
    return matrix.astype(jnp.bfloat16)

def phase_angle(shift_now, half_bit, angles, freq_count):
    angle_pos = (half_bit * angles + jnp.arange(angles, dtype=jnp.int32)).astype(jnp.float32)
    across = (angle_pos + 0.5) / (2.0 * angles) - 0.5
    ranges = (jnp.arange(freq_count, dtype=jnp.int32) + freq_count).astype(jnp.float32) / freq_count
    return 2.0 * math.pi * shift_now * across[:, None] * ranges[None, :]

def rotate(real_part, imag_part, cosine, sine_map):
    return (cosine * real_part - sine_map * imag_part, cosine * imag_part + sine_map * real_part)

def reference(raw, taps, weights, shifts):
    tile_count = N_GRP * N_BAND
    half_len = ANGLES // 2
    samples = raw.reshape(2, NF, tile_count, PULSE_DEV)
    profile = (jnp.einsum('cftq,cfds->dtqs', samples.astype(jnp.float32), range_table(NF).astype(jnp.float32)) * (1.0 / math.sqrt(NF))).astype(jnp.bfloat16)
    images = (jnp.einsum('dacq,ctqr->tdar', beam_table(ANGLES, PULSE_DEV).astype(jnp.float32), profile.astype(jnp.float32)) * (1.0 / math.sqrt(PULSE_DEV))).astype(jnp.bfloat16)
    band_bits = N_BAND.bit_length() - 1
    numbers = np.arange(tile_count)
    for section_no in range(LEVELS):
        bit_pos = section_no if section_no < BAND_LEVELS else band_bits + section_no - BAND_LEVELS
        bit_mask = 1 << bit_pos
        merged = images
        for half_bit in (0, 1):
            chosen = numbers[numbers >> bit_pos & 1 == half_bit]
            start = half_bit * half_len
            lower_half = images[chosen & ~bit_mask][:, :, start:start + half_len]
            upper_half = images[chosen | bit_mask][:, :, start:start + half_len]
            matrix = interp_matrix(taps[section_no, half_bit], weights[section_no, half_bit], half_len).astype(jnp.float32)
            low_prod = jnp.einsum('jk,tcks->tcjs', matrix, lower_half.astype(jnp.float32))
            up_prod = jnp.einsum('jk,tcks->tcjs', matrix, upper_half.astype(jnp.float32))
            angle_map = phase_angle(shifts[section_no], half_bit, ANGLES, NF)
            cosine = jnp.cos(angle_map)
            sine_map = jnp.sin(angle_map)
            low_re, low_im = rotate(low_prod[:, 0], low_prod[:, 1], cosine, sine_map)
            up_re, up_im = rotate(up_prod[:, 0], up_prod[:, 1], cosine, -sine_map)
            merged_block = (jnp.stack([low_re + up_re, low_im + up_im], axis=1) * inv_root_two).astype(jnp.bfloat16)
            merged = merged.at[chosen].set(merged_block)
        images = merged
    return jnp.transpose(images, (1, 0, 2, 3)).reshape(2, tile_count * ANGLES, NF)
```

```python
import functools
import math

import jax
import jax.numpy as jnp
import numpy as np
from jax import lax
from jax.experimental import pallas as pl
from jax.experimental.pallas import tpu as pltpu
from jax.sharding import PartitionSpec as P

MESH = pl.DeviceIdType.MESH
NF = 256
ANGLES = 512
HALF = 256
LEVELS = 5
WIN = (24, 40, 72, 144, 256)
OUT = (40, 72, 144, 256, 512)
STACK = (4, 4, 2, 1, 1)
CHUNKS = 4


def chain(h, lesser, greater):
    low, starts = 0, [0] * LEVELS
    for level in range(LEVELS - 2, -1, -1):
        low = greater((h[level + 1] * HALF + low) // 2 - 1, 0)
        starts[level] = lesser(low, HALF - WIN[level])
    return starts


def beam_rows():
    rows = []
    for w in range(32):
        h = [w >> (4 - i) & 1 for i in range(5)]
        first = h[0] * HALF + chain(h, min, max)[0]
        rows.append(first + np.arange(WIN[0]))
    return np.concatenate(rows)


def tables():
    a = beam_rows()
    q = np.arange(512)
    beam = 2.0 * np.pi * (a[:, None] * q[None, :] % ANGLES) / ANGLES
    beam = np.concatenate([np.cos(beam), np.sin(beam)], axis=1)
    f = np.arange(NF)
    turn = 2.0 * np.pi * (f[:, None] * f[None, :] % NF) / NF
    cos = jnp.asarray(np.cos(turn), jnp.bfloat16)
    sin = jnp.asarray(np.sin(turn), jnp.bfloat16)
    real = jnp.concatenate([cos, -sin], axis=1)
    imag = jnp.concatenate([sin, cos], axis=1)
    both = jnp.stack([real.reshape(4, 8, 8, 512), imag.reshape(4, 8, 8, 512)], axis=2)
    both = both.transpose(1, 0, 2, 3, 4).reshape(8, 64, 512)
    return jnp.asarray(beam, jnp.bfloat16), both * jnp.bfloat16(1.0 / 16.0)


COS = np.polynomial.chebyshev.Chebyshev.interpolate(
    lambda s: np.cos(2 * np.pi * np.sqrt(s)), 7, domain=[0.0, 0.25]
).convert(kind=np.polynomial.Polynomial).coef
SIN = np.polynomial.chebyshev.Chebyshev.interpolate(
    lambda s: np.sinc(2 * np.sqrt(s)) * 2 * np.pi, 7, domain=[0.0, 0.25]
).convert(kind=np.polynomial.Polynomial).coef


def poly(coef, s):
    out = jnp.full_like(s, float(coef[-1]))
    for value in coef[-2::-1]:
        out = out * s + float(value)
    return out


def kernel(
    raw, taps, weights, shifts, beam_hbm, range_hbm, out,
    zbuf, beam, rtab, rexp, rawk, sbuf, rbuf, ph_c, ph_s, p0, p1, p2, p3, p4, x1, x2, x3, x4,
    zsend, zrecv, ssend, srecv, local,
):
    grp = lax.axis_index("grp")
    band = lax.axis_index("band")
    zh, x, c = band // 8, (band // 2) % 4, band % 2
    zl, y = grp // 4, grp % 4
    h = [c, x % 2, x // 2, y % 2, y // 2]
    mine = h[0] * 16 + h[1] * 8 + h[2] * 4 + h[3] * 2 + h[4]
    starts = chain(h, jnp.minimum, jnp.maximum)
    my_slot = (x * 2 + c) * 4 + y

    def zpeer(dz):
        return {"band": ((zh + dz) % 4) * 8 + x * 2 + c, "grp": grp}

    def near(o):
        xo, co, yo = (x + o // 2 % 4) % 4, (c + o % 2) % 2, (y + o // 8) % 4
        w = co * 16 + (xo % 2) * 8 + (xo // 2) * 4 + (yo % 2) * 2 + yo // 2
        return {"band": zh * 8 + xo * 2 + co, "grp": zl * 4 + yo}, w

    own = []
    own.append(pltpu.make_async_copy(beam_hbm, beam, local.at[0]))
    own.append(pltpu.make_async_copy(range_hbm, rtab, local.at[1]))
    for k in range(CHUNKS):
        own.append(
            pltpu.make_async_copy(
                raw.at[:, :, pl.ds(pl.multiple_of(zh * 4096 + k * 1024, 1024), 1024)],
                zbuf.at[k, zh],
                local.at[2 + k],
            )
        )
    for cp in own:
        cp.start()

    barrier = pltpu.get_barrier_semaphore()
    for dz in (2, 1, 3):
        pl.semaphore_signal(barrier, inc=1, device_id=zpeer(dz), device_id_type=MESH)

    def greet(o, carry):
        pl.semaphore_signal(barrier, inc=1, device_id=near(o)[0], device_id_type=MESH)
        return carry

    lax.fori_loop(1, 32, greet, 0)

    at = 0
    bases = []
    for level in range(LEVELS):
        rows, stack = OUT[level], STACK[level]
        if level < LEVELS - 1:
            first = h[level + 1] * HALF + starts[level + 1]
        else:
            first = 0
        j = (lax.broadcasted_iota(jnp.int32, (rows, 256), 0) + (h[level] * 512 + first)).astype(jnp.float32)
        r = lax.broadcasted_iota(jnp.int32, (rows, 256), 1).astype(jnp.float32)
        across = (j + 0.5) * (1.0 / 1024.0) - 0.5
        turns = (shifts[level] * across) * ((r + 256.0) * (1.0 / 256.0))
        turns = turns - jnp.round(turns)
        square = turns * turns
        cos = poly(COS, square) * math.sqrt(0.5)
        sin = poly(SIN, square) * turns * math.sqrt(0.5)
        for n in range(stack):
            ph_c[at + n * rows : at + (n + 1) * rows, :] = cos
            ph_s[at + n * rows : at + (n + 1) * rows, :] = sin
        bases.append(at)
        at += rows * stack

    pl.semaphore_wait(barrier, 34)

    zcopies = []
    for k in range(CHUNKS):
        for dz in (2, 1, 3):
            to = (zh + dz) % 4
            cp = pltpu.make_async_remote_copy(
                src_ref=raw.at[:, :, pl.ds(pl.multiple_of(to * 4096 + k * 1024, 1024), 1024)],
                dst_ref=zbuf.at[k, zh],
                send_sem=zsend.at[k, dz],
                recv_sem=zrecv.at[k, dz],
                device_id=zpeer(dz),
                device_id_type=MESH,
            )
            cp.start()
            zcopies.append(cp)

    for level, pm in enumerate((p0, p1, p2, p3, p4)):
        rows, stack, wide = OUT[level], STACK[level], WIN[level]
        mp = -(-rows * stack // 128) * 128
        kp = -(-wide * stack // 128) * 128
        tp = taps[level, h[level]]
        wt = weights[level, h[level]]
        if level < LEVELS - 1:
            first = h[level + 1] * HALF + starts[level + 1]
            lane = lax.broadcasted_iota(jnp.int32, (4, 512), 1)
            tp_all = jnp.full((4, 512), -1, jnp.int32)
            wt_all = jnp.zeros((4, 512), jnp.float32)
            for n in range(stack):
                turn = (512 + n * rows - first) % 512
                here = (lane >= n * rows) & (lane < (n + 1) * rows)
                tp_all = jnp.where(here, pltpu.roll(tp, turn, 1) + (n * wide - starts[level]), tp_all)
                wt_all = jnp.where(here, pltpu.roll(wt, turn, 1), wt_all)
            tp, wt = tp_all, wt_all
        ids = lax.broadcasted_iota(jnp.int32, (kp, mp), 0)
        total = jnp.zeros((kp, mp), jnp.float32)
        for s in range(4):
            total = total + jnp.where(tp[s : s + 1, :mp] == ids, wt[s : s + 1, :mp], 0.0)
        pm[...] = total.T[: rows * stack, : wide * stack].astype(jnp.bfloat16)

    own[1].wait()
    rexp[...] = jnp.zeros_like(rexp)
    for s in range(8):
        rexp[s * 128 : s * 128 + 64, 0:512] = rtab[s]
        rexp[s * 128 + 64 : s * 128 + 128, 512:1024] = rtab[s]

    def rotate(prod, level):
        base, rows = bases[level], OUT[level] * STACK[level]
        cos = ph_c[base : base + rows, :]
        sin = ph_s[base : base + rows, :]
        first, second = prod[:, 0:512], prod[:, 512:1024]
        add = first + second
        sub = first - second
        re = cos * add[:, :256] - sin * sub[:, 256:]
        im = cos * add[:, 256:] + sin * sub[:, :256]
        return re, im

    def dot(a, b):
        return jnp.dot(a, b, preferred_element_type=jnp.float32)

    def block_copy(k, o):
        dev, w = near(o)
        return pltpu.make_async_remote_copy(
            src_ref=sbuf.at[k, w],
            dst_ref=rbuf.at[k, my_slot],
            send_sem=ssend.at[k],
            recv_sem=srecv.at[k],
            device_id=dev,
            device_id_type=MESH,
        )

    def all_of(k):
        return pltpu.make_async_remote_copy(
            src_ref=sbuf.at[k, pl.ds(0, 31)],
            dst_ref=rbuf.at[k, pl.ds(0, 31)],
            send_sem=ssend.at[k],
            recv_sem=srecv.at[k],
            device_id=near(1)[0],
            device_id_type=MESH,
        )

    def send(k):
        own[2 + k].wait()
        for i in range(3):
            zcopies[k * 3 + i].wait_recv()
        for t in range(2):
            part = zbuf[k, :, :, :, t * 512 : (t + 1) * 512]
            real, imag = part[:, 0], part[:, 1]
            plain = jnp.stack([real, imag], axis=1).reshape(64, 512)
            turned = jnp.stack([imag, -real], axis=1).reshape(64, 512)
            rawk[t * 64 : (t + 1) * 64, 0:512] = plain
            rawk[t * 64 : (t + 1) * 64, 512:1024] = turned
        prod = lax.dot_general(
            beam[...], rawk[...], (((1,), (1,)), ((), ())), preferred_element_type=jnp.float32
        )
        prod = (prod * (1.0 / math.sqrt(512.0))).astype(jnp.bfloat16)
        sbuf[k] = prod.reshape(32, WIN[0], 128)

        def push(o, carry):
            block_copy(k, o).start()
            return carry

        lax.fori_loop(1, 32, push, 0)
        rbuf[k, my_slot] = sbuf[k, mine]

    def take(k):
        all_of(k).wait_recv()
        lhs = jnp.concatenate(
            [rbuf[k, s * 4 : s * 4 + 4].reshape(4 * WIN[0], 128) for s in range(8)], axis=1
        )
        sub0 = dot(lhs, rexp[...]).astype(jnp.bfloat16)
        re, im = rotate(dot(p0[...], sub0), 0)
        half = k % 2 * 512
        x1[k // 2, :, half : half + 256] = re.astype(jnp.bfloat16)
        x1[k // 2, :, half + 256 : half + 512] = im.astype(jnp.bfloat16)
        if k % 2 == 1:
            m = k // 2
            re, im = rotate(dot(p1[...], x1[m]), 1)
            for yh in range(2):
                x2[yh, :, m * 512 : m * 512 + 256] = re[yh * 144 : yh * 144 + 144].astype(jnp.bfloat16)
                x2[yh, :, m * 512 + 256 : m * 512 + 512] = im[yh * 144 : yh * 144 + 144].astype(jnp.bfloat16)

    own[0].wait()
    send(0)
    for k in range(1, CHUNKS):
        send(k)
        take(k - 1)
    take(CHUNKS - 1)
    for yh in range(2):
        re, im = rotate(dot(p2[...], x2[yh]), 2)
        for yb in range(2):
            x3[yh, :, yb * 512 : yb * 512 + 256] = re[yb * 144 : yb * 144 + 144].astype(jnp.bfloat16)
            x3[yh, :, yb * 512 + 256 : yb * 512 + 512] = im[yb * 144 : yb * 144 + 144].astype(jnp.bfloat16)
    for yh in range(2):
        re, im = rotate(dot(p3[...], x3[yh]), 3)
        x4[:, yh * 512 : yh * 512 + 256] = re.astype(jnp.bfloat16)
        x4[:, yh * 512 + 256 : yh * 512 + 512] = im.astype(jnp.bfloat16)
    re, im = rotate(dot(p4[...], x4[...]), 4)
    out[0] = re.astype(jnp.bfloat16)
    out[1] = im.astype(jnp.bfloat16)

    for cp in zcopies:
        cp.wait_send()
    for k in range(CHUNKS):
        all_of(k).wait_send()


def on_device(raw, taps, weights, shifts):
    beam, rtab = tables()
    rows = sum(o * s for o, s in zip(OUT, STACK))
    anyspace = pl.BlockSpec(memory_space=pl.ANY)
    vmem = pl.BlockSpec(memory_space=pltpu.VMEM)
    bf = jnp.bfloat16
    return pl.pallas_call(
        kernel,
        name="backproject",
        out_shape=jax.ShapeDtypeStruct((2, ANGLES, NF), bf),
        in_specs=[anyspace, vmem, vmem, pl.BlockSpec(memory_space=pltpu.SMEM), anyspace, anyspace],
        out_specs=vmem,
        scratch_shapes=[
            pltpu.VMEM((CHUNKS, 4, 2, 8, 1024), bf),
            pltpu.VMEM((768, 1024), bf),
            pltpu.VMEM((8, 64, 512), bf),
            pltpu.VMEM((1024, 1024), bf),
            pltpu.VMEM((128, 1024), bf),
            pltpu.VMEM((CHUNKS, 32, WIN[0], 128), bf),
            pltpu.VMEM((CHUNKS, 32, WIN[0], 128), bf),
            pltpu.VMEM((rows, 256), jnp.float32),
            pltpu.VMEM((rows, 256), jnp.float32),
        ]
        + [pltpu.VMEM((OUT[i] * STACK[i], WIN[i] * STACK[i]), bf) for i in range(LEVELS)]
        + [
            pltpu.VMEM((2, 160, 1024), bf),
            pltpu.VMEM((2, 144, 1024), bf),
            pltpu.VMEM((2, 144, 1024), bf),
            pltpu.VMEM((256, 1024), bf),
            pltpu.SemaphoreType.DMA((CHUNKS, 4)),
            pltpu.SemaphoreType.DMA((CHUNKS, 4)),
            pltpu.SemaphoreType.DMA((CHUNKS,)),
            pltpu.SemaphoreType.DMA((CHUNKS,)),
            pltpu.SemaphoreType.DMA((6,)),
        ],
        compiler_params=pltpu.CompilerParams(
            collective_id=0, has_side_effects=True, vmem_limit_bytes=56 << 20
        ),
    )(raw, taps, weights, shifts, beam, rtab)


def solution(mesh):
    return jax.shard_map(
        on_device,
        mesh=mesh,
        in_specs=(P(None, "band", "grp"), P(), P(), P()),
        out_specs=P(None, ("grp", "band"), None),
        check_vma=False,
    )
```

```python
import functools
import math

import jax
import jax.numpy as jnp
import numpy as np
from jax import lax
from jax.experimental import pallas as pl
from jax.experimental.pallas import tpu as pltpu
from jax.sharding import PartitionSpec as P

MESH = pl.DeviceIdType.MESH
NF = 256
ANGLES = 512
HALF = 256
LEVELS = 5
WIN = (24, 40, 72, 144, 256)
OUT = (40, 72, 144, 256, 512)
STACK = (4, 4, 2, 1, 1)
CHUNKS = 4


def chain(h, lesser, greater):
    low, starts = 0, [0] * LEVELS
    for level in range(LEVELS - 2, -1, -1):
        low = greater((h[level + 1] * HALF + low) // 2 - 1, 0)
        starts[level] = lesser(low, HALF - WIN[level])
    return starts


def beam_rows():
    rows = []
    for w in range(32):
        h = [w >> (4 - i) & 1 for i in range(5)]
        first = h[0] * HALF + chain(h, min, max)[0]
        rows.append(first + np.arange(WIN[0]))
    return np.concatenate(rows)


def tables():
    a = beam_rows()
    q = np.arange(512)
    beam = 2.0 * np.pi * (a[:, None] * q[None, :] % ANGLES) / ANGLES
    beam = np.concatenate([np.cos(beam), np.sin(beam)], axis=1)
    f = np.arange(NF)
    turn = 2.0 * np.pi * (f[:, None] * f[None, :] % NF) / NF
    cos = jnp.asarray(np.cos(turn), jnp.bfloat16)
    sin = jnp.asarray(np.sin(turn), jnp.bfloat16)
    real = jnp.concatenate([cos, -sin], axis=1)
    imag = jnp.concatenate([sin, cos], axis=1)
    both = jnp.stack([real.reshape(4, 8, 8, 512), imag.reshape(4, 8, 8, 512)], axis=2)
    both = both.transpose(1, 0, 2, 3, 4).reshape(8, 64, 512)
    return jnp.asarray(beam, jnp.bfloat16), both * jnp.bfloat16(1.0 / 16.0)


COS = np.polynomial.chebyshev.Chebyshev.interpolate(
    lambda s: np.cos(2 * np.pi * np.sqrt(s)), 7, domain=[0.0, 0.25]
).convert(kind=np.polynomial.Polynomial).coef
SIN = np.polynomial.chebyshev.Chebyshev.interpolate(
    lambda s: np.sinc(2 * np.sqrt(s)) * 2 * np.pi, 7, domain=[0.0, 0.25]
).convert(kind=np.polynomial.Polynomial).coef


def poly(coef, s):
    out = jnp.full_like(s, float(coef[-1]))
    for value in coef[-2::-1]:
        out = out * s + float(value)
    return out


def kernel(
    raw, taps_hbm, weights_hbm, shifts_hbm, beam_hbm, range_hbm, out,
    taps, weights, shifts, zbuf, beam, rtab, rexp, rawk, sbuf, rbuf, ph_c, ph_s, p0, p1, p2, p3, p4, x1, x2, x3, x4,
    zsend, zrecv, ssend, srecv, local, zready, xyready,
):
    grp = lax.axis_index("grp")
    band = lax.axis_index("band")
    zh, x, c = band // 8, (band // 2) % 4, band % 2
    zl, y = grp // 4, grp % 4
    h = [c, x % 2, x // 2, y % 2, y // 2]
    mine = h[0] * 16 + h[1] * 8 + h[2] * 4 + h[3] * 2 + h[4]
    starts = chain(h, jnp.minimum, jnp.maximum)
    my_slot = (x * 2 + c) * 4 + y

    def zpeer(dz):
        return {"band": ((zh + dz) % 4) * 8 + x * 2 + c, "grp": grp}

    def near(o):
        xo, co, yo = (x + 2 + o // 2 % 4) % 4, (c + 1 + o % 2) % 2, (y + 2 + o // 8) % 4
        w = co * 16 + (xo % 2) * 8 + (xo // 2) * 4 + (yo % 2) * 2 + yo // 2
        return {"band": zh * 8 + xo * 2 + co, "grp": zl * 4 + yo}, w

    own = []
    own.append(pltpu.make_async_copy(beam_hbm, beam, local.at[0]))
    own.append(pltpu.make_async_copy(range_hbm, rtab, local.at[1]))
    for k in range(CHUNKS):
        own.append(
            pltpu.make_async_copy(
                raw.at[:, :, pl.ds(pl.multiple_of(zh * 4096 + k * 1024, 1024), 1024)],
                zbuf.at[k, zh],
                local.at[2 + k],
            )
        )
    small = [
        pltpu.make_async_copy(shifts_hbm, shifts, local.at[6]),
        pltpu.make_async_copy(taps_hbm, taps, local.at[7]),
        pltpu.make_async_copy(weights_hbm, weights, local.at[8]),
    ]
    barrier = pltpu.get_barrier_semaphore()
    partner = {"band": zh * 8 + x * 2 + 1 - c, "grp": grp}
    for dz in (2, 1, 3):
        to = {"band": ((zh + dz) % 4) * 8 + x * 2, "grp": grp}
        pl.semaphore_signal(barrier, inc=1, device_id=to, device_id_type=MESH)
    pl.semaphore_signal(barrier, inc=1, device_id=partner, device_id_type=MESH)

    def greet(o, carry):
        to = {"band": zh * 8 + (x + o % 4) % 4 * 2 + 1, "grp": zl * 4 + (y + o // 4) % 4}
        pl.semaphore_signal(barrier, inc=1, device_id=to, device_id_type=MESH)
        return carry

    lax.fori_loop(1, 16, greet, 0)

    @pl.when(c == 0)
    def _():
        pl.semaphore_wait(barrier, 7)
        pl.semaphore_signal(zready, inc=1, device_id=partner, device_id_type=MESH)

    @pl.when(c == 1)
    def _():
        pl.semaphore_wait(zready, 1)

    zcopies = []
    for k in range(CHUNKS):
        for dz in (2, 1, 3):
            to = (zh + dz) % 4
            cp = pltpu.make_async_remote_copy(
                src_ref=raw.at[:, :, pl.ds(pl.multiple_of(to * 4096 + k * 1024, 1024), 1024)],
                dst_ref=zbuf.at[k, zh],
                send_sem=zsend.at[k, dz],
                recv_sem=zrecv.at[k, dz],
                device_id=zpeer(dz),
                device_id_type=MESH,
            )
            cp.start()
            zcopies.append(cp)

    for cp in small + own:
        cp.start()
    for cp in small:
        cp.wait()

    at = 0
    bases = []
    for level in range(LEVELS):
        rows, stack = OUT[level], STACK[level]
        if level < LEVELS - 1:
            first = h[level + 1] * HALF + starts[level + 1]
        else:
            first = 0
        j = (lax.broadcasted_iota(jnp.int32, (rows, 256), 0) + (h[level] * 512 + first)).astype(jnp.float32)
        r = lax.broadcasted_iota(jnp.int32, (rows, 256), 1).astype(jnp.float32)
        across = (j + 0.5) * (1.0 / 1024.0) - 0.5
        turns = (shifts[level] * across) * ((r + 256.0) * (1.0 / 256.0))
        turns = turns - jnp.round(turns)
        square = turns * turns
        cos = poly(COS, square) * math.sqrt(0.5)
        sin = poly(SIN, square) * turns * math.sqrt(0.5)
        for n in range(stack):
            ph_c[at + n * rows : at + (n + 1) * rows, :] = cos
            ph_s[at + n * rows : at + (n + 1) * rows, :] = sin
        bases.append(at)
        at += rows * stack

    for level, pm in enumerate((p0, p1, p2, p3, p4)):
        rows, stack, wide = OUT[level], STACK[level], WIN[level]
        mp = -(-rows * stack // 128) * 128
        kp = -(-wide * stack // 128) * 128
        tp = taps[level, h[level]]
        wt = weights[level, h[level]]
        if level < LEVELS - 1:
            first = h[level + 1] * HALF + starts[level + 1]
            lane = lax.broadcasted_iota(jnp.int32, (4, 512), 1)
            tp_all = jnp.full((4, 512), -1, jnp.int32)
            wt_all = jnp.zeros((4, 512), jnp.float32)
            for n in range(stack):
                turn = (512 + n * rows - first) % 512
                here = (lane >= n * rows) & (lane < (n + 1) * rows)
                tp_all = jnp.where(here, pltpu.roll(tp, turn, 1) + (n * wide - starts[level]), tp_all)
                wt_all = jnp.where(here, pltpu.roll(wt, turn, 1), wt_all)
            tp, wt = tp_all, wt_all
        ids = lax.broadcasted_iota(jnp.int32, (kp, mp), 0)
        total = jnp.zeros((kp, mp), jnp.float32)
        for s in range(4):
            total = total + jnp.where(tp[s : s + 1, :mp] == ids, wt[s : s + 1, :mp], 0.0)
        pm[...] = total.T[: rows * stack, : wide * stack].astype(jnp.bfloat16)

    own[1].wait()
    rexp[...] = jnp.zeros_like(rexp)
    for s in range(8):
        rexp[s * 128 : s * 128 + 64, 0:512] = rtab[s]
        rexp[s * 128 + 64 : s * 128 + 128, 512:1024] = rtab[s]

    def rotate(prod, level):
        base, rows = bases[level], OUT[level] * STACK[level]
        cos = ph_c[base : base + rows, :]
        sin = ph_s[base : base + rows, :]
        first, second = prod[:, 0:512], prod[:, 512:1024]
        add = first + second
        sub = first - second
        re = cos * add[:, :256] - sin * sub[:, 256:]
        im = cos * add[:, 256:] + sin * sub[:, :256]
        return re, im

    def dot(a, b):
        return jnp.dot(a, b, preferred_element_type=jnp.float32)

    def block_copy(k, o):
        dev, w = near(o)
        return pltpu.make_async_remote_copy(
            src_ref=sbuf.at[k, w],
            dst_ref=rbuf.at[k, my_slot],
            send_sem=ssend.at[k],
            recv_sem=srecv.at[k],
            device_id=dev,
            device_id_type=MESH,
        )

    def all_of(k):
        return pltpu.make_async_remote_copy(
            src_ref=sbuf.at[k, pl.ds(0, 31)],
            dst_ref=rbuf.at[k, pl.ds(0, 31)],
            send_sem=ssend.at[k],
            recv_sem=srecv.at[k],
            device_id=near(0)[0],
            device_id_type=MESH,
        )

    def send(k):
        own[2 + k].wait()
        for i in range(3):
            zcopies[k * 3 + i].wait_recv()
        for t in range(2):
            part = zbuf[k, :, :, :, t * 512 : (t + 1) * 512]
            real, imag = part[:, 0], part[:, 1]
            plain = jnp.stack([real, imag], axis=1).reshape(64, 512)
            turned = jnp.stack([imag, -real], axis=1).reshape(64, 512)
            rawk[t * 64 : (t + 1) * 64, 0:512] = plain
            rawk[t * 64 : (t + 1) * 64, 512:1024] = turned
        prod = lax.dot_general(
            beam[...], rawk[...], (((1,), (1,)), ((), ())), preferred_element_type=jnp.float32
        )
        prod = (prod * (1.0 / math.sqrt(512.0))).astype(jnp.bfloat16)
        sbuf[k] = prod.reshape(32, WIN[0], 128)

        def push(o, carry):
            block_copy(k, o).start()
            return carry

        lax.fori_loop(0, 21, push, 0)
        lax.fori_loop(22, 32, push, 0)
        rbuf[k, my_slot] = sbuf[k, mine]

    def take(k):
        all_of(k).wait_recv()
        lhs = jnp.concatenate(
            [rbuf[k, s * 4 : s * 4 + 4].reshape(4 * WIN[0], 128) for s in range(8)], axis=1
        )
        sub0 = dot(lhs, rexp[...]).astype(jnp.bfloat16)
        re, im = rotate(dot(p0[...], sub0), 0)
        half = k % 2 * 512
        x1[k // 2, :, half : half + 256] = re.astype(jnp.bfloat16)
        x1[k // 2, :, half + 256 : half + 512] = im.astype(jnp.bfloat16)
        if k % 2 == 1:
            m = k // 2
            re, im = rotate(dot(p1[...], x1[m]), 1)
            for yh in range(2):
                x2[yh, :, m * 512 : m * 512 + 256] = re[yh * 144 : yh * 144 + 144].astype(jnp.bfloat16)
                x2[yh, :, m * 512 + 256 : m * 512 + 512] = im[yh * 144 : yh * 144 + 144].astype(jnp.bfloat16)

    @pl.when(c == 0)
    def _():
        pl.semaphore_wait(xyready, 1)

    @pl.when(c == 1)
    def _():
        pl.semaphore_wait(barrier, 31)
        pl.semaphore_signal(xyready, inc=1, device_id=partner, device_id_type=MESH)

    own[0].wait()
    send(0)
    for k in range(1, CHUNKS):
        send(k)
        take(k - 1)
    take(CHUNKS - 1)
    for yh in range(2):
        re, im = rotate(dot(p2[...], x2[yh]), 2)
        for yb in range(2):
            x3[yh, :, yb * 512 : yb * 512 + 256] = re[yb * 144 : yb * 144 + 144].astype(jnp.bfloat16)
            x3[yh, :, yb * 512 + 256 : yb * 512 + 512] = im[yb * 144 : yb * 144 + 144].astype(jnp.bfloat16)
    for yh in range(2):
        re, im = rotate(dot(p3[...], x3[yh]), 3)
        x4[:, yh * 512 : yh * 512 + 256] = re.astype(jnp.bfloat16)
        x4[:, yh * 512 + 256 : yh * 512 + 512] = im.astype(jnp.bfloat16)
    re, im = rotate(dot(p4[...], x4[...]), 4)
    out[0] = re.astype(jnp.bfloat16)
    out[1] = im.astype(jnp.bfloat16)

    for cp in zcopies:
        cp.wait_send()
    for k in range(CHUNKS):
        all_of(k).wait_send()


def on_device(raw, taps, weights, shifts):
    beam, rtab = tables()
    rows = sum(o * s for o, s in zip(OUT, STACK))
    hbm = pl.BlockSpec(memory_space=pltpu.HBM)
    vmem = pl.BlockSpec(memory_space=pltpu.VMEM)
    bf = jnp.bfloat16
    return pl.pallas_call(
        kernel,
        name="backproject",
        out_shape=jax.ShapeDtypeStruct((2, ANGLES, NF), bf),
        in_specs=[hbm] * 6,
        out_specs=vmem,
        scratch_shapes=[
            pltpu.VMEM((LEVELS, 2, 4, 512), jnp.int32),
            pltpu.VMEM((LEVELS, 2, 4, 512), jnp.float32),
            pltpu.SMEM((LEVELS,), jnp.float32),
            pltpu.VMEM((CHUNKS, 4, 2, 8, 1024), bf),
            pltpu.VMEM((768, 1024), bf),
            pltpu.VMEM((8, 64, 512), bf),
            pltpu.VMEM((1024, 1024), bf),
            pltpu.VMEM((128, 1024), bf),
            pltpu.VMEM((CHUNKS, 32, WIN[0], 128), bf),
            pltpu.VMEM((CHUNKS, 32, WIN[0], 128), bf),
            pltpu.VMEM((rows, 256), jnp.float32),
            pltpu.VMEM((rows, 256), jnp.float32),
        ]
        + [pltpu.VMEM((OUT[i] * STACK[i], WIN[i] * STACK[i]), bf) for i in range(LEVELS)]
        + [
            pltpu.VMEM((2, 160, 1024), bf),
            pltpu.VMEM((2, 144, 1024), bf),
            pltpu.VMEM((2, 144, 1024), bf),
            pltpu.VMEM((256, 1024), bf),
            pltpu.SemaphoreType.DMA((CHUNKS, 4)),
            pltpu.SemaphoreType.DMA((CHUNKS, 4)),
            pltpu.SemaphoreType.DMA((CHUNKS,)),
            pltpu.SemaphoreType.DMA((CHUNKS,)),
            pltpu.SemaphoreType.DMA((9,)),
            pltpu.SemaphoreType.REGULAR,
            pltpu.SemaphoreType.REGULAR,
        ],
        compiler_params=pltpu.CompilerParams(
            collective_id=0, has_side_effects=True, vmem_limit_bytes=32 << 20
        ),
    )(*(pltpu.with_memory_space_constraint(a, pltpu.HBM) for a in (raw, taps, weights, shifts, beam, rtab)))


def solution(mesh):
    return jax.shard_map(
        on_device,
        mesh=mesh,
        in_specs=(P(None, "band", "grp"), P(), P(), P()),
        out_specs=P(None, ("grp", "band"), None),
        check_vma=False,
    )
```

```python
import functools
import math

import jax
import jax.numpy as jnp
import numpy as np
from jax import lax
from jax.experimental import pallas as pl
from jax.experimental.pallas import tpu as pltpu
from jax.sharding import PartitionSpec as P

MESH = pl.DeviceIdType.MESH
NF = 256
ANGLES = 512
HALF = 256
LEVELS = 5
WIN = (24, 40, 72, 144, 256)
OUT = (40, 72, 144, 256, 512)
STACK = (4, 4, 2, 1, 1)
CHUNKS = 4


def chain(h, lesser, greater):
    low, starts = 0, [0] * LEVELS
    for level in range(LEVELS - 2, -1, -1):
        low = greater((h[level + 1] * HALF + low) // 2 - 1, 0)
        starts[level] = lesser(low, HALF - WIN[level])
    return starts


def beam_rows():
    rows = []
    for w in range(32):
        h = [w >> (4 - i) & 1 for i in range(5)]
        first = h[0] * HALF + chain(h, min, max)[0]
        rows.append(first + np.arange(WIN[0]))
    return np.concatenate(rows)


def tables():
    a = beam_rows()
    q = np.arange(512)
    beam = 2.0 * np.pi * (a[:, None] * q[None, :] % ANGLES) / ANGLES
    beam = np.concatenate([np.cos(beam), np.sin(beam)], axis=1)
    f = np.arange(NF)
    turn = 2.0 * np.pi * (f[:, None] * f[None, :] % NF) / NF
    cos = jnp.asarray(np.cos(turn), jnp.bfloat16)
    sin = jnp.asarray(np.sin(turn), jnp.bfloat16)
    real = jnp.concatenate([cos, -sin], axis=1)
    imag = jnp.concatenate([sin, cos], axis=1)
    both = jnp.stack([real.reshape(4, 8, 8, 512), imag.reshape(4, 8, 8, 512)], axis=2)
    both = both.transpose(1, 0, 2, 3, 4).reshape(512, 512)
    return jnp.asarray(beam, jnp.bfloat16), both * jnp.bfloat16(1.0 / 16.0)


COS = np.polynomial.chebyshev.Chebyshev.interpolate(
    lambda s: np.cos(2 * np.pi * np.sqrt(s)), 7, domain=[0.0, 0.25]
).convert(kind=np.polynomial.Polynomial).coef
SIN = np.polynomial.chebyshev.Chebyshev.interpolate(
    lambda s: np.sinc(2 * np.sqrt(s)) * 2 * np.pi, 7, domain=[0.0, 0.25]
).convert(kind=np.polynomial.Polynomial).coef


def poly(coef, s):
    out = jnp.full_like(s, float(coef[-1]))
    for value in coef[-2::-1]:
        out = out * s + float(value)
    return out


def kernel(
    raw, taps_hbm, weights_hbm, shifts_hbm, beam_hbm, range_hbm, out,
    taps, weights, shifts, zbuf, beam, rtab, rawk, sbuf, rbuf, ph_c, ph_s, p0, p1, p2, p3, p4, x1, x2, x3, x4,
    zsend, zrecv, ssend, srecv, local, known, xyready,
):
    grp = lax.axis_index("grp")
    band = lax.axis_index("band")
    zh, x, c = band // 8, (band // 2) % 4, band % 2
    zl, y = grp // 4, grp % 4
    h = [c, x % 2, x // 2, y % 2, y // 2]
    mine = h[0] * 16 + h[1] * 8 + h[2] * 4 + h[3] * 2 + h[4]
    starts = chain(h, jnp.minimum, jnp.maximum)
    my_slot = (x * 2 + c) * 4 + y

    def near(o):
        xo, co, yo = (x + 2 + o // 2 % 4) % 4, (c + 1 + o % 2) % 2, (y + 2 + o // 8) % 4
        w = co * 16 + (xo % 2) * 8 + (xo // 2) * 4 + (yo % 2) * 2 + yo // 2
        return {"band": zh * 8 + xo * 2 + co, "grp": zl * 4 + yo}, w

    own = []
    own.append(pltpu.make_async_copy(beam_hbm, beam, local.at[0]))
    own.append(pltpu.make_async_copy(range_hbm, rtab, local.at[1]))
    for k in range(CHUNKS):
        own.append(
            pltpu.make_async_copy(
                raw.at[:, :, pl.ds(pl.multiple_of(zh * 4096 + k * 1024, 1024), 1024)],
                zbuf.at[k, zh],
                local.at[2 + k],
            )
        )
    small = [
        pltpu.make_async_copy(shifts_hbm, shifts, local.at[6]),
        pltpu.make_async_copy(taps_hbm, taps, local.at[7]),
        pltpu.make_async_copy(weights_hbm, weights, local.at[8]),
    ]
    for cp in small + own:
        cp.start()

    barrier = pltpu.get_barrier_semaphore()

    def by_zh(values):
        picked = values[0]
        for i in range(1, 4):
            picked = jnp.where(zh == i, values[i], picked)
        return picked

    def signal(sem, to):
        pl.semaphore_signal(sem, inc=1, device_id=to, device_id_type=MESH)

    def column(zo, co):
        return {"band": zo * 8 + x * 2 + co, "grp": grp}

    partner = column(zh, 1 - c)
    soon = ((1, 0), (3, 0), (2, 0), (2, 1))
    late = ((3, 1), (2, 3))
    for pairs, core in ((soon, 0), (late, 1)):
        for hears, speaks in pairs:

            @pl.when(zh == speaks)
            def _(hears=hears, core=core):
                signal(barrier, column(hears, core))

    signal(barrier, partner)

    def greet(o, carry):
        signal(barrier, {"band": zh * 8 + (x + o % 4) % 4 * 2 + 1, "grp": zl * 4 + (y + o // 4) % 4})
        return carry

    lax.fori_loop(1, 16, greet, 0)

    def tell(pairs):
        for hears, speaks in pairs:

            @pl.when(zh == hears)
            def _(hears=hears, speaks=speaks):
                pl.semaphore_signal(known.at[speaks], inc=1)
                signal(known.at[speaks], partner)
                for co in range(2):
                    signal(known.at[hears], column(speaks, co))

    @pl.when(c == 0)
    def _():
        pl.semaphore_wait(barrier, by_zh((1, 3, 5, 3)))
        tell(soon)

    def hear_rest():
        pl.semaphore_wait(barrier, by_zh((31, 31, 33, 33)))
        tell(late)
        signal(xyready, partner)

    order = ((1, 3, 2), (0, 2, 3), (0, 1, 3), (0, 1, 2))

    dests = [by_zh([o[p] for o in order]) for p in range(3)]

    def meet(p):
        pl.semaphore_wait(known.at[dests[p]], 1)

    def zcopy(p, k):
        return pltpu.make_async_remote_copy(
            src_ref=raw.at[:, :, pl.ds(pl.multiple_of(dests[p] * 4096 + k * 1024, 1024), 1024)],
            dst_ref=zbuf.at[k, zh],
            send_sem=zsend.at[k, p],
            recv_sem=zrecv.at[k, zh],
            device_id=column(dests[p], c),
            device_id_type=MESH,
        )

    def zsend_one(p, k):
        zcopy(p, k).start()

    meet(0)
    for k in range(CHUNKS):
        zsend_one(0, k)
    pl.when((c == 1) & (zh != 2))(hear_rest)
    meet(1)
    for k in range(2):
        zsend_one(1, k)
    pl.when((c == 1) & (zh == 2))(hear_rest)
    for cp in small:
        cp.wait()

    at = 0
    bases = []
    for level in range(LEVELS):
        rows, stack = OUT[level], STACK[level]
        if level < LEVELS - 1:
            first = h[level + 1] * HALF + starts[level + 1]
        else:
            first = 0
        j = (lax.broadcasted_iota(jnp.int32, (rows, 256), 0) + (h[level] * 512 + first)).astype(jnp.float32)
        r = lax.broadcasted_iota(jnp.int32, (rows, 256), 1).astype(jnp.float32)
        across = (j + 0.5) * (1.0 / 1024.0) - 0.5
        turns = (shifts[level] * across) * ((r + 256.0) * (1.0 / 256.0))
        turns = turns - jnp.round(turns)
        square = turns * turns
        cos = poly(COS, square) * math.sqrt(0.5)
        sin = poly(SIN, square) * turns * math.sqrt(0.5)
        for n in range(stack):
            ph_c[at + n * rows : at + (n + 1) * rows, :] = cos
            ph_s[at + n * rows : at + (n + 1) * rows, :] = sin
        bases.append(at)
        at += rows * stack

    meet(2)
    for p, k in ((2, 0), (2, 1), (1, 2), (2, 2)):
        zsend_one(p, k)
    eager = (zl == 1) | (zl == 2)
    rest = [(p, k) for k in range(3, CHUNKS) for p in (1, 2)]

    @pl.when(eager)
    def _():
        for p, k in rest:
            zcopy(p, k).start()


    for level, pm in enumerate((p0, p1, p2, p3, p4)):
        rows, stack, wide = OUT[level], STACK[level], WIN[level]
        mp = -(-rows * stack // 128) * 128
        kp = -(-wide * stack // 128) * 128
        tp = taps[level, h[level]]
        wt = weights[level, h[level]]
        if level < LEVELS - 1:
            first = h[level + 1] * HALF + starts[level + 1]
            lane = lax.broadcasted_iota(jnp.int32, (4, 512), 1)
            tp_all = jnp.full((4, 512), -1, jnp.int32)
            wt_all = jnp.zeros((4, 512), jnp.float32)
            for n in range(stack):
                turn = (512 + n * rows - first) % 512
                here = (lane >= n * rows) & (lane < (n + 1) * rows)
                tp_all = jnp.where(here, pltpu.roll(tp, turn, 1) + (n * wide - starts[level]), tp_all)
                wt_all = jnp.where(here, pltpu.roll(wt, turn, 1), wt_all)
            tp, wt = tp_all, wt_all
        ids = lax.broadcasted_iota(jnp.int32, (kp, mp), 0)
        total = jnp.zeros((kp, mp), jnp.float32)
        for s in range(4):
            total = total + jnp.where(tp[s : s + 1, :mp] == ids, wt[s : s + 1, :mp], 0.0)
        pm[...] = total.T[: rows * stack, : wide * stack].astype(jnp.bfloat16)

    def rotate(prod, level):
        base, rows = bases[level], OUT[level] * STACK[level]
        cos = ph_c[base : base + rows, :]
        sin = ph_s[base : base + rows, :]
        first, second = prod[:, 0:512], prod[:, 512:1024]
        add = first + second
        sub = first - second
        re = cos * add[:, :256] - sin * sub[:, 256:]
        im = cos * add[:, 256:] + sin * sub[:, :256]
        return re, im

    def dot(a, b):
        return jnp.dot(a, b, preferred_element_type=jnp.float32)

    def block_copy(k, o):
        dev, w = near(o)
        return pltpu.make_async_remote_copy(
            src_ref=sbuf.at[k, w],
            dst_ref=rbuf.at[k, my_slot],
            send_sem=ssend.at[k],
            recv_sem=srecv.at[k],
            device_id=dev,
            device_id_type=MESH,
        )

    def all_of(k):
        return pltpu.make_async_remote_copy(
            src_ref=sbuf.at[k, pl.ds(0, 31)],
            dst_ref=rbuf.at[k, pl.ds(0, 31)],
            send_sem=ssend.at[k],
            recv_sem=srecv.at[k],
            device_id=near(0)[0],
            device_id_type=MESH,
        )

    def send(k):
        own[2 + k].wait()
        for i in range(1, 4):
            came = (zh + i) % 4
            pltpu.make_async_remote_copy(
                src_ref=zbuf.at[k, came],
                dst_ref=zbuf.at[k, came],
                send_sem=zsend.at[k, 0],
                recv_sem=zrecv.at[k, came],
                device_id=column(came, c),
                device_id_type=MESH,
            ).wait_recv()
        if k + 3 < CHUNKS:

            @pl.when(jnp.logical_not(eager))
            def _():
                for p in (1, 2):
                    zcopy(p, k + 3).start()

        for t in range(2):
            part = zbuf[k, :, :, :, t * 512 : (t + 1) * 512]
            real, imag = part[:, 0], part[:, 1]
            plain = jnp.stack([real, imag], axis=1).reshape(64, 512)
            turned = jnp.stack([imag, -real], axis=1).reshape(64, 512)
            rawk[t * 64 : (t + 1) * 64, 0:512] = plain
            rawk[t * 64 : (t + 1) * 64, 512:1024] = turned
        prod = lax.dot_general(
            beam[...], rawk[...], (((1,), (1,)), ((), ())), preferred_element_type=jnp.float32
        )
        prod = (prod * (1.0 / math.sqrt(512.0))).astype(jnp.bfloat16)
        sbuf[k] = prod.reshape(32, WIN[0], 128)

        def push(o, carry):
            block_copy(k, o).start()
            return carry

        lax.fori_loop(0, 21, push, 0)
        lax.fori_loop(22, 32, push, 0)
        rbuf[k, my_slot] = sbuf[k, mine]

    def take(k):
        all_of(k).wait_recv()
        came = [rbuf[k, s * 4 : s * 4 + 4].reshape(4 * WIN[0], 128) for s in range(8)]
        lhs = jnp.concatenate(
            [
                jnp.concatenate([piece[:, t * 64 : t * 64 + 64] for piece in came], axis=1)
                for t in range(2)
            ],
            axis=0,
        )
        sub0 = dot(lhs, rtab[...]).astype(jnp.bfloat16)
        sub0 = jnp.concatenate([sub0[: 4 * WIN[0]], sub0[4 * WIN[0] :]], axis=1)
        re, im = rotate(dot(p0[...], sub0), 0)
        half = k % 2 * 512
        x1[k // 2, :, half : half + 256] = re.astype(jnp.bfloat16)
        x1[k // 2, :, half + 256 : half + 512] = im.astype(jnp.bfloat16)
        if k % 2 == 1:
            m = k // 2
            re, im = rotate(dot(p1[...], x1[m]), 1)
            for yh in range(2):
                x2[yh, :, m * 512 : m * 512 + 256] = re[yh * 144 : yh * 144 + 144].astype(jnp.bfloat16)
                x2[yh, :, m * 512 + 256 : m * 512 + 512] = im[yh * 144 : yh * 144 + 144].astype(jnp.bfloat16)

    @pl.when(c == 0)
    def _():
        pl.semaphore_wait(xyready, 1)

    own[0].wait()
    own[1].wait()
    send(0)
    for k in range(1, CHUNKS):
        send(k)
        take(k - 1)
    take(CHUNKS - 1)
    for yh in range(2):
        re, im = rotate(dot(p2[...], x2[yh]), 2)
        for yb in range(2):
            x3[yh, :, yb * 512 : yb * 512 + 256] = re[yb * 144 : yb * 144 + 144].astype(jnp.bfloat16)
            x3[yh, :, yb * 512 + 256 : yb * 512 + 512] = im[yb * 144 : yb * 144 + 144].astype(jnp.bfloat16)
    for yh in range(2):
        re, im = rotate(dot(p3[...], x3[yh]), 3)
        x4[:, yh * 512 : yh * 512 + 256] = re.astype(jnp.bfloat16)
        x4[:, yh * 512 + 256 : yh * 512 + 512] = im.astype(jnp.bfloat16)
    re, im = rotate(dot(p4[...], x4[...]), 4)
    out[0] = re.astype(jnp.bfloat16)
    out[1] = im.astype(jnp.bfloat16)

    for p in range(3):
        for k in range(CHUNKS):
            zcopy(p, k).wait_send()
    for k in range(CHUNKS):
        all_of(k).wait_send()


def on_device(raw, taps, weights, shifts):
    beam, rtab = tables()
    rows = sum(o * s for o, s in zip(OUT, STACK))
    hbm = pl.BlockSpec(memory_space=pltpu.HBM)
    vmem = pl.BlockSpec(memory_space=pltpu.VMEM)
    bf = jnp.bfloat16
    return pl.pallas_call(
        kernel,
        name="backproject",
        out_shape=jax.ShapeDtypeStruct((2, ANGLES, NF), bf),
        in_specs=[hbm] * 6,
        out_specs=vmem,
        scratch_shapes=[
            pltpu.VMEM((LEVELS, 2, 4, 512), jnp.int32),
            pltpu.VMEM((LEVELS, 2, 4, 512), jnp.float32),
            pltpu.SMEM((LEVELS,), jnp.float32),
            pltpu.VMEM((CHUNKS, 4, 2, 8, 1024), bf),
            pltpu.VMEM((768, 1024), bf),
            pltpu.VMEM((512, 512), bf),
            pltpu.VMEM((128, 1024), bf),
            pltpu.VMEM((CHUNKS, 32, WIN[0], 128), bf),
            pltpu.VMEM((CHUNKS, 32, WIN[0], 128), bf),
            pltpu.VMEM((rows, 256), jnp.float32),
            pltpu.VMEM((rows, 256), jnp.float32),
        ]
        + [pltpu.VMEM((OUT[i] * STACK[i], WIN[i] * STACK[i]), bf) for i in range(LEVELS)]
        + [
            pltpu.VMEM((2, 160, 1024), bf),
            pltpu.VMEM((2, 144, 1024), bf),
            pltpu.VMEM((2, 144, 1024), bf),
            pltpu.VMEM((256, 1024), bf),
            pltpu.SemaphoreType.DMA((CHUNKS, 4)),
            pltpu.SemaphoreType.DMA((CHUNKS, 4)),
            pltpu.SemaphoreType.DMA((CHUNKS,)),
            pltpu.SemaphoreType.DMA((CHUNKS,)),
            pltpu.SemaphoreType.DMA((9,)),
            pltpu.SemaphoreType.REGULAR((4,)),
            pltpu.SemaphoreType.REGULAR,
        ],
        compiler_params=pltpu.CompilerParams(
            collective_id=0, has_side_effects=True, vmem_limit_bytes=32 << 20
        ),
    )(*(pltpu.with_memory_space_constraint(a, pltpu.HBM) for a in (raw, taps, weights, shifts, beam, rtab)))


def solution(mesh):
    return jax.shard_map(
        on_device,
        mesh=mesh,
        in_specs=(P(None, "band", "grp"), P(), P(), P()),
        out_specs=P(None, ("grp", "band"), None),
        check_vma=False,
    )
```

```python
import functools
import math

import jax
import jax.numpy as jnp
import numpy as np
from jax import lax
from jax.experimental import pallas as pl
from jax.experimental.pallas import tpu as pltpu
from jax.sharding import PartitionSpec as P

MESH = pl.DeviceIdType.MESH
NF = 256
ANGLES = 512
HALF = 256
LEVELS = 5
WIN = (24, 40, 72, 144, 256)
OUT = (40, 72, 144, 256, 512)
STACK = (4, 4, 2, 1, 1)
CHUNKS = 4


def chain(h, lesser, greater):
    low, starts = 0, [0] * LEVELS
    for level in range(LEVELS - 2, -1, -1):
        low = greater((h[level + 1] * HALF + low) // 2 - 1, 0)
        starts[level] = lesser(low, HALF - WIN[level])
    return starts


def beam_rows():
    rows = []
    for w in range(32):
        h = [w >> (4 - i) & 1 for i in range(5)]
        first = h[0] * HALF + chain(h, min, max)[0]
        rows.append(first + np.arange(WIN[0]))
    return np.concatenate(rows)


def tables():
    a = beam_rows()
    q = np.arange(512)
    beam = 2.0 * np.pi * (a[:, None] * q[None, :] % ANGLES) / ANGLES
    beam = np.concatenate([np.cos(beam), np.sin(beam)], axis=1)
    f = np.arange(NF)
    turn = 2.0 * np.pi * (f[:, None] * f[None, :] % NF) / NF
    cos = jnp.asarray(np.cos(turn), jnp.bfloat16)
    sin = jnp.asarray(np.sin(turn), jnp.bfloat16)
    real = jnp.concatenate([cos, -sin], axis=1)
    imag = jnp.concatenate([sin, cos], axis=1)
    both = jnp.stack([real.reshape(4, 8, 8, 512), imag.reshape(4, 8, 8, 512)], axis=2)
    both = both.transpose(1, 0, 2, 3, 4).reshape(512, 512)
    return jnp.asarray(beam, jnp.bfloat16), both * jnp.bfloat16(1.0 / 16.0)


COS = np.polynomial.chebyshev.Chebyshev.interpolate(
    lambda s: np.cos(2 * np.pi * np.sqrt(s)), 7, domain=[0.0, 0.25]
).convert(kind=np.polynomial.Polynomial).coef
SIN = np.polynomial.chebyshev.Chebyshev.interpolate(
    lambda s: np.sinc(2 * np.sqrt(s)) * 2 * np.pi, 7, domain=[0.0, 0.25]
).convert(kind=np.polynomial.Polynomial).coef


def poly(coef, s):
    out = jnp.full_like(s, float(coef[-1]))
    for value in coef[-2::-1]:
        out = out * s + float(value)
    return out


def kernel(
    raw, taps_hbm, weights_hbm, shifts_hbm, beam_hbm, range_hbm, out,
    taps, weights, shifts, zbuf, beam, rtab, rawk, sbuf, rbuf, ph_c, ph_s, p0, p1, p2, p3, p4, x1, x2, x3, x4,
    zsend, zrecv, ssend, srecv, local, known, xyready,
):
    grp = lax.axis_index("grp")
    band = lax.axis_index("band")
    zh, x, c = band // 8, (band // 2) % 4, band % 2
    zl, y = grp // 4, grp % 4
    h = [c, x % 2, x // 2, y % 2, y // 2]
    mine = h[0] * 16 + h[1] * 8 + h[2] * 4 + h[3] * 2 + h[4]
    starts = chain(h, jnp.minimum, jnp.maximum)
    my_slot = (x * 2 + c) * 4 + y

    bands = [[zh * 8 + (x + dx) % 4 * 2 + (c + dc) % 2 for dc in range(2)] for dx in range(4)]
    grps = [zl * 4 + (y + dy) % 4 for dy in range(4)]
    w_c = [(c + dc) % 2 * 16 for dc in range(2)]
    w_x = [(x + dx) % 2 * 8 + (x + dx) % 4 // 2 * 4 for dx in range(4)]
    w_y = [(y + dy) % 2 * 2 + (y + dy) % 4 // 2 for dy in range(4)]
    others = [(dx, dc, dy) for dx in range(4) for dc in range(2) for dy in range(4)][1:]
    others.sort(key=lambda o: -min(o[0], 4 - o[0]) - min(o[2], 4 - o[2]))

    def near(other):
        dx, dc, dy = other
        return {"band": bands[dx][dc], "grp": grps[dy]}, w_c[dc] + w_x[dx] + w_y[dy]

    own = []
    own.append(pltpu.make_async_copy(beam_hbm, beam, local.at[0]))
    own.append(pltpu.make_async_copy(range_hbm, rtab, local.at[1]))
    for k in range(CHUNKS):
        own.append(
            pltpu.make_async_copy(
                raw.at[:, :, pl.ds(pl.multiple_of(zh * 4096 + k * 1024, 1024), 1024)],
                zbuf.at[k, zh],
                local.at[2 + k],
            )
        )
    small = [
        pltpu.make_async_copy(shifts_hbm, shifts, local.at[6]),
        pltpu.make_async_copy(taps_hbm, taps, local.at[7]),
        pltpu.make_async_copy(weights_hbm, weights, local.at[8]),
    ]
    for cp in small + own:
        cp.start()

    barrier = pltpu.get_barrier_semaphore()

    def by_zh(values):
        picked = values[0]
        for i in range(1, 4):
            picked = jnp.where(zh == i, values[i], picked)
        return picked

    def signal(sem, to):
        pl.semaphore_signal(sem, inc=1, device_id=to, device_id_type=MESH)

    def column(zo, co):
        return {"band": zo * 8 + x * 2 + co, "grp": grp}

    partner = column(zh, 1 - c)
    soon = ((1, 0), (3, 0), (2, 0), (2, 1))
    late = ((3, 1), (2, 3))
    for pairs, core in ((soon, 0), (late, 1)):
        for hears, speaks in pairs:

            @pl.when(zh == speaks)
            def _(hears=hears, core=core):
                signal(barrier, column(hears, core))

    signal(barrier, partner)

    def greet(o, carry):
        signal(barrier, {"band": zh * 8 + (x + o % 4) % 4 * 2 + 1, "grp": zl * 4 + (y + o // 4) % 4})
        return carry

    lax.fori_loop(1, 16, greet, 0)

    def tell(pairs):
        for hears, speaks in pairs:

            @pl.when(zh == hears)
            def _(hears=hears, speaks=speaks):
                pl.semaphore_signal(known.at[speaks], inc=1)
                signal(known.at[speaks], partner)
                for co in range(2):
                    signal(known.at[hears], column(speaks, co))

    @pl.when(c == 0)
    def _():
        pl.semaphore_wait(barrier, by_zh((1, 3, 5, 3)))
        tell(soon)

    def hear_rest():
        pl.semaphore_wait(barrier, by_zh((31, 31, 33, 33)))
        tell(late)
        signal(xyready, partner)

    order = ((1, 3, 2), (0, 2, 3), (0, 1, 3), (0, 1, 2))

    dests = [by_zh([o[p] for o in order]) for p in range(3)]

    def meet(p):
        pl.semaphore_wait(known.at[dests[p]], 1)

    def zcopy(p, k):
        return pltpu.make_async_remote_copy(
            src_ref=raw.at[:, :, pl.ds(pl.multiple_of(dests[p] * 4096 + k * 1024, 1024), 1024)],
            dst_ref=zbuf.at[k, zh],
            send_sem=zsend.at[k, p],
            recv_sem=zrecv.at[k, zh],
            device_id=column(dests[p], c),
            device_id_type=MESH,
        )

    def zsend_one(p, k):
        zcopy(p, k).start()

    meet(0)
    zsend_one(0, 0)
    zsend_one(0, 1)
    zsend_one(0, 2)
    pl.when((c == 1) & (zh != 2))(hear_rest)
    meet(1)
    zsend_one(1, 0)
    zsend_one(1, 1)
    pl.when((c == 1) & (zh == 2))(hear_rest)
    for cp in small:
        cp.wait()

    at = 0
    bases = []
    for level in range(LEVELS):
        rows, stack = OUT[level], STACK[level]
        if level < LEVELS - 1:
            first = h[level + 1] * HALF + starts[level + 1]
        else:
            first = 0
        j = (lax.broadcasted_iota(jnp.int32, (rows, 256), 0) + (h[level] * 512 + first)).astype(jnp.float32)
        r = lax.broadcasted_iota(jnp.int32, (rows, 256), 1).astype(jnp.float32)
        across = (j + 0.5) * (1.0 / 1024.0) - 0.5
        turns = (shifts[level] * across) * ((r + 256.0) * (1.0 / 256.0))
        turns = turns - jnp.round(turns)
        square = turns * turns
        cos = poly(COS, square) * math.sqrt(0.5)
        sin = poly(SIN, square) * turns * math.sqrt(0.5)
        for n in range(stack):
            ph_c[at + n * rows : at + (n + 1) * rows, :] = cos
            ph_s[at + n * rows : at + (n + 1) * rows, :] = sin
        bases.append(at)
        at += rows * stack

    meet(2)
    zsend_one(2, 0)
    zsend_one(2, 1)

    for level, pm in enumerate((p0, p1, p2, p3, p4)):
        rows, stack, wide = OUT[level], STACK[level], WIN[level]
        mp = -(-rows * stack // 128) * 128
        kp = -(-wide * stack // 128) * 128
        tp = taps[level, h[level]]
        wt = weights[level, h[level]]
        if level < LEVELS - 1:
            first = h[level + 1] * HALF + starts[level + 1]
            lane = lax.broadcasted_iota(jnp.int32, (4, 512), 1)
            tp_all = jnp.full((4, 512), -1, jnp.int32)
            wt_all = jnp.zeros((4, 512), jnp.float32)
            for n in range(stack):
                turn = (512 + n * rows - first) % 512
                here = (lane >= n * rows) & (lane < (n + 1) * rows)
                tp_all = jnp.where(here, pltpu.roll(tp, turn, 1) + (n * wide - starts[level]), tp_all)
                wt_all = jnp.where(here, pltpu.roll(wt, turn, 1), wt_all)
            tp, wt = tp_all, wt_all
        ids = lax.broadcasted_iota(jnp.int32, (kp, mp), 0)
        total = jnp.zeros((kp, mp), jnp.float32)
        for s in range(4):
            total = total + jnp.where(tp[s : s + 1, :mp] == ids, wt[s : s + 1, :mp], 0.0)
        pm[...] = total.T[: rows * stack, : wide * stack].astype(jnp.bfloat16)

    pl.when(zl != 0)(lambda: pl.delay(2500))
    zsend_one(1, 2)
    zsend_one(2, 2)
    pl.delay(2500)
    pl.when(zl != 0)(lambda: pl.delay(2500))
    zsend_one(0, 3)
    zsend_one(1, 3)
    zsend_one(2, 3)

    def rotate(prod, level):
        base, rows = bases[level], OUT[level] * STACK[level]
        cos = ph_c[base : base + rows, :]
        sin = ph_s[base : base + rows, :]
        first, second = prod[:, 0:512], prod[:, 512:1024]
        add = first + second
        sub = first - second
        re = cos * add[:, :256] - sin * sub[:, 256:]
        im = cos * add[:, 256:] + sin * sub[:, :256]
        return re, im

    def dot(a, b):
        return jnp.dot(a, b, preferred_element_type=jnp.float32)

    def block_copy(k, o):
        dev, w = near(o)
        return pltpu.make_async_remote_copy(
            src_ref=sbuf.at[k, w],
            dst_ref=rbuf.at[k, my_slot],
            send_sem=ssend.at[k],
            recv_sem=srecv.at[k],
            device_id=dev,
            device_id_type=MESH,
        )

    def all_of(k):
        return pltpu.make_async_remote_copy(
            src_ref=sbuf.at[k, pl.ds(0, 31)],
            dst_ref=rbuf.at[k, pl.ds(0, 31)],
            send_sem=ssend.at[k],
            recv_sem=srecv.at[k],
            device_id=near(others[0])[0],
            device_id_type=MESH,
        )

    def send(k):
        own[2 + k].wait()
        for i in range(1, 4):
            came = (zh + i) % 4
            pltpu.make_async_remote_copy(
                src_ref=zbuf.at[k, came],
                dst_ref=zbuf.at[k, came],
                send_sem=zsend.at[k, 0],
                recv_sem=zrecv.at[k, came],
                device_id=column(came, c),
                device_id_type=MESH,
            ).wait_recv()
        for t in range(2):
            part = zbuf[k, :, :, :, t * 512 : (t + 1) * 512]
            real, imag = part[:, 0], part[:, 1]
            plain = jnp.stack([real, imag], axis=1).reshape(64, 512)
            turned = jnp.stack([imag, -real], axis=1).reshape(64, 512)
            rawk[t * 64 : (t + 1) * 64, 0:512] = plain
            rawk[t * 64 : (t + 1) * 64, 512:1024] = turned
        prod = lax.dot_general(
            beam[...], rawk[...], (((1,), (1,)), ((), ())), preferred_element_type=jnp.float32
        )
        prod = (prod * (1.0 / math.sqrt(512.0))).astype(jnp.bfloat16)
        sbuf[k] = prod.reshape(32, WIN[0], 128)

        for other in others:
            block_copy(k, other).start()
        rbuf[k, my_slot] = sbuf[k, mine]

    def take(k):
        all_of(k).wait_recv()
        came = [rbuf[k, s * 4 : s * 4 + 4].reshape(4 * WIN[0], 128) for s in range(8)]
        lhs = jnp.concatenate(
            [
                jnp.concatenate([piece[:, t * 64 : t * 64 + 64] for piece in came], axis=1)
                for t in range(2)
            ],
            axis=0,
        )
        sub0 = dot(lhs, rtab[...]).astype(jnp.bfloat16)
        sub0 = jnp.concatenate([sub0[: 4 * WIN[0]], sub0[4 * WIN[0] :]], axis=1)
        re, im = rotate(dot(p0[...], sub0), 0)
        half = k % 2 * 512
        x1[k // 2, :, half : half + 256] = re.astype(jnp.bfloat16)
        x1[k // 2, :, half + 256 : half + 512] = im.astype(jnp.bfloat16)
        if k % 2 == 1:
            m = k // 2
            re, im = rotate(dot(p1[...], x1[m]), 1)
            for yh in range(2):
                x2[yh, :, m * 512 : m * 512 + 256] = re[yh * 144 : yh * 144 + 144].astype(jnp.bfloat16)
                x2[yh, :, m * 512 + 256 : m * 512 + 512] = im[yh * 144 : yh * 144 + 144].astype(jnp.bfloat16)

    @pl.when(c == 0)
    def _():
        pl.semaphore_wait(xyready, 1)

    own[0].wait()
    own[1].wait()
    send(0)
    for k in range(1, CHUNKS):
        send(k)
        take(k - 1)
    take(CHUNKS - 1)
    for yh in range(2):
        re, im = rotate(dot(p2[...], x2[yh]), 2)
        for yb in range(2):
            x3[yh, :, yb * 512 : yb * 512 + 256] = re[yb * 144 : yb * 144 + 144].astype(jnp.bfloat16)
            x3[yh, :, yb * 512 + 256 : yb * 512 + 512] = im[yb * 144 : yb * 144 + 144].astype(jnp.bfloat16)
    for yh in range(2):
        re, im = rotate(dot(p3[...], x3[yh]), 3)
        x4[:, yh * 512 : yh * 512 + 256] = re.astype(jnp.bfloat16)
        x4[:, yh * 512 + 256 : yh * 512 + 512] = im.astype(jnp.bfloat16)
    re, im = rotate(dot(p4[...], x4[...]), 4)
    out[0] = re.astype(jnp.bfloat16)
    out[1] = im.astype(jnp.bfloat16)

    for p in range(3):
        for k in range(CHUNKS):
            zcopy(p, k).wait_send()
    for k in range(CHUNKS):
        all_of(k).wait_send()


def on_device(raw, taps, weights, shifts):
    beam, rtab = tables()
    rows = sum(o * s for o, s in zip(OUT, STACK))
    hbm = pl.BlockSpec(memory_space=pltpu.HBM)
    vmem = pl.BlockSpec(memory_space=pltpu.VMEM)
    bf = jnp.bfloat16
    return pl.pallas_call(
        kernel,
        name="backproject",
        out_shape=jax.ShapeDtypeStruct((2, ANGLES, NF), bf),
        in_specs=[hbm] * 6,
        out_specs=vmem,
        scratch_shapes=[
            pltpu.VMEM((LEVELS, 2, 4, 512), jnp.int32),
            pltpu.VMEM((LEVELS, 2, 4, 512), jnp.float32),
            pltpu.SMEM((LEVELS,), jnp.float32),
            pltpu.VMEM((CHUNKS, 4, 2, 8, 1024), bf),
            pltpu.VMEM((768, 1024), bf),
            pltpu.VMEM((512, 512), bf),
            pltpu.VMEM((128, 1024), bf),
            pltpu.VMEM((CHUNKS, 32, WIN[0], 128), bf),
            pltpu.VMEM((CHUNKS, 32, WIN[0], 128), bf),
            pltpu.VMEM((rows, 256), jnp.float32),
            pltpu.VMEM((rows, 256), jnp.float32),
        ]
        + [pltpu.VMEM((OUT[i] * STACK[i], WIN[i] * STACK[i]), bf) for i in range(LEVELS)]
        + [
            pltpu.VMEM((2, 160, 1024), bf),
            pltpu.VMEM((2, 144, 1024), bf),
            pltpu.VMEM((2, 144, 1024), bf),
            pltpu.VMEM((256, 1024), bf),
            pltpu.SemaphoreType.DMA((CHUNKS, 4)),
            pltpu.SemaphoreType.DMA((CHUNKS, 4)),
            pltpu.SemaphoreType.DMA((CHUNKS,)),
            pltpu.SemaphoreType.DMA((CHUNKS,)),
            pltpu.SemaphoreType.DMA((9,)),
            pltpu.SemaphoreType.REGULAR((4,)),
            pltpu.SemaphoreType.REGULAR,
        ],
        compiler_params=pltpu.CompilerParams(
            collective_id=0, has_side_effects=True, vmem_limit_bytes=32 << 20
        ),
    )(*(pltpu.with_memory_space_constraint(a, pltpu.HBM) for a in (raw, taps, weights, shifts, beam, rtab)))


def solution(mesh):
    return jax.shard_map(
        on_device,
        mesh=mesh,
        in_specs=(P(None, "band", "grp"), P(), P(), P()),
        out_specs=P(None, ("grp", "band"), None),
        check_vma=False,
    )
```

```python
import functools
import math

import jax
import jax.numpy as jnp
import numpy as np
from jax import lax
from jax.experimental import pallas as pl
from jax.experimental.pallas import tpu as pltpu
from jax.sharding import PartitionSpec as P

MESH = pl.DeviceIdType.MESH
NF = 256
ANGLES = 512
HALF = 256
LEVELS = 5
WIN = (24, 40, 72, 144, 256)
OUT = (40, 72, 144, 256, 512)
STACK = (4, 4, 2, 1, 1)
CHUNKS = 4


def chain(h, lesser, greater):
    low, starts = 0, [0] * LEVELS
    for level in range(LEVELS - 2, -1, -1):
        low = greater((h[level + 1] * HALF + low) // 2 - 1, 0)
        starts[level] = lesser(low, HALF - WIN[level])
    return starts


def beam_rows():
    rows = []
    for w in range(32):
        h = [w >> (4 - i) & 1 for i in range(5)]
        first = h[0] * HALF + chain(h, min, max)[0]
        rows.append(first + np.arange(WIN[0]))
    return np.concatenate(rows)


def tables():
    a = beam_rows()
    q = np.arange(512)
    beam = 2.0 * np.pi * (a[:, None] * q[None, :] % ANGLES) / ANGLES
    beam = np.concatenate([np.cos(beam), np.sin(beam)], axis=1)
    f = np.arange(NF)
    turn = 2.0 * np.pi * (f[:, None] * f[None, :] % NF) / NF
    cos = jnp.asarray(np.cos(turn), jnp.bfloat16)
    sin = jnp.asarray(np.sin(turn), jnp.bfloat16)
    real = jnp.concatenate([cos, -sin], axis=1)
    imag = jnp.concatenate([sin, cos], axis=1)
    both = jnp.stack([real.reshape(4, 8, 8, 512), imag.reshape(4, 8, 8, 512)], axis=2)
    both = both.transpose(1, 0, 2, 3, 4).reshape(512, 512)
    return jnp.asarray(beam, jnp.bfloat16), both * jnp.bfloat16(1.0 / 16.0)


COS = np.polynomial.chebyshev.Chebyshev.interpolate(
    lambda s: np.cos(2 * np.pi * np.sqrt(s)), 7, domain=[0.0, 0.25]
).convert(kind=np.polynomial.Polynomial).coef
SIN = np.polynomial.chebyshev.Chebyshev.interpolate(
    lambda s: np.sinc(2 * np.sqrt(s)) * 2 * np.pi, 7, domain=[0.0, 0.25]
).convert(kind=np.polynomial.Polynomial).coef


def poly(coef, s):
    out = jnp.full_like(s, float(coef[-1]))
    for value in coef[-2::-1]:
        out = out * s + float(value)
    return out


def kernel(
    raw, taps_hbm, weights_hbm, shifts_hbm, beam_hbm, range_hbm, out,
    taps, weights, shifts, zbuf, beam, rtab, rawk, sbuf, rbuf, ph_c, ph_s, p0, p1, p2, p3, p4, x1, x2, x3, x4,
    zsend, zrecv, ssend, srecv, local, known, xyready,
):
    grp = lax.axis_index("grp")
    band = lax.axis_index("band")
    zh, x, c = band // 8, (band // 2) % 4, band % 2
    zl, y = grp // 4, grp % 4
    h = [c, x % 2, x // 2, y % 2, y // 2]
    mine = h[0] * 16 + h[1] * 8 + h[2] * 4 + h[3] * 2 + h[4]
    starts = chain(h, jnp.minimum, jnp.maximum)
    my_slot = (x * 2 + c) * 4 + y

    bands = [[zh * 8 + (x + dx) % 4 * 2 + (c + dc) % 2 for dc in range(2)] for dx in range(4)]
    grps = [zl * 4 + (y + dy) % 4 for dy in range(4)]
    w_c = [(c + dc) % 2 * 16 for dc in range(2)]
    w_x = [(x + dx) % 2 * 8 + (x + dx) % 4 // 2 * 4 for dx in range(4)]
    w_y = [(y + dy) % 2 * 2 + (y + dy) % 4 // 2 for dy in range(4)]
    others = [(dx, dc, dy) for dx in range(4) for dc in range(2) for dy in range(4)][1:]
    others.sort(key=lambda o: -min(o[0], 4 - o[0]) - min(o[2], 4 - o[2]))

    def near(other):
        dx, dc, dy = other
        return {"band": bands[dx][dc], "grp": grps[dy]}, w_c[dc] + w_x[dx] + w_y[dy]

    own = []
    own.append(pltpu.make_async_copy(beam_hbm, beam, local.at[0]))
    own.append(pltpu.make_async_copy(range_hbm, rtab, local.at[1]))
    for k in range(CHUNKS):
        own.append(
            pltpu.make_async_copy(
                raw.at[:, :, pl.ds(pl.multiple_of(zh * 4096 + k * 1024, 1024), 1024)],
                zbuf.at[k, zh],
                local.at[2 + k],
            )
        )
    small = [
        pltpu.make_async_copy(shifts_hbm, shifts, local.at[6]),
        pltpu.make_async_copy(taps_hbm, taps, local.at[7]),
        pltpu.make_async_copy(weights_hbm, weights, local.at[8]),
    ]
    barrier = pltpu.get_barrier_semaphore()

    def by_zh(values):
        picked = values[0]
        for i in range(1, 4):
            picked = jnp.where(zh == i, values[i], picked)
        return picked

    def signal(sem, to):
        pl.semaphore_signal(sem, inc=1, device_id=to, device_id_type=MESH)

    def column(zo, co):
        return {"band": zo * 8 + x * 2 + co, "grp": grp}

    partner = column(zh, 1 - c)
    soon = ((1, 0), (3, 0), (2, 0), (2, 1))
    late = ((3, 1), (2, 3))
    for pairs, core in ((soon, 0), (late, 1)):
        for hears, speaks in pairs:

            @pl.when(zh == speaks)
            def _(hears=hears, core=core):
                signal(barrier, column(hears, core))

    signal(barrier, partner)

    def greet(o, carry):
        signal(barrier, {"band": zh * 8 + (x + o % 4) % 4 * 2 + 1, "grp": zl * 4 + (y + o // 4) % 4})
        return carry

    lax.fori_loop(1, 16, greet, 0)

    for cp in small + own:
        cp.start()

    def tell(pairs):
        for hears, speaks in pairs:

            @pl.when(zh == hears)
            def _(hears=hears, speaks=speaks):
                pl.semaphore_signal(known.at[speaks], inc=1)
                signal(known.at[speaks], partner)
                for co in range(2):
                    signal(known.at[hears], column(speaks, co))

    @pl.when(c == 0)
    def _():
        pl.semaphore_wait(barrier, by_zh((1, 3, 5, 3)))
        tell(soon)

    def hear_rest():
        pl.semaphore_wait(barrier, by_zh((31, 31, 33, 33)))
        tell(late)
        signal(xyready, partner)

    order = ((1, 3, 2), (0, 2, 3), (0, 1, 3), (0, 1, 2))

    dests = [by_zh([o[p] for o in order]) for p in range(3)]

    def meet(p):
        pl.semaphore_wait(known.at[dests[p]], 1)

    def zcopy(p, k):
        return pltpu.make_async_remote_copy(
            src_ref=raw.at[:, :, pl.ds(pl.multiple_of(dests[p] * 4096 + k * 1024, 1024), 1024)],
            dst_ref=zbuf.at[k, zh],
            send_sem=zsend.at[k, p],
            recv_sem=zrecv.at[k, zh],
            device_id=column(dests[p], c),
            device_id_type=MESH,
        )

    def zsend_one(p, k):
        zcopy(p, k).start()

    meet(0)
    zsend_one(0, 0)
    zsend_one(0, 1)
    zsend_one(0, 2)
    pl.when((c == 1) & (zh != 2))(hear_rest)
    meet(1)
    zsend_one(1, 0)
    zsend_one(1, 1)
    pl.when((c == 1) & (zh == 2))(hear_rest)
    for cp in small:
        cp.wait()

    at = 0
    bases = []
    for level in range(LEVELS):
        rows, stack = OUT[level], STACK[level]
        if level < LEVELS - 1:
            first = h[level + 1] * HALF + starts[level + 1]
        else:
            first = 0
        j = (lax.broadcasted_iota(jnp.int32, (rows, 256), 0) + (h[level] * 512 + first)).astype(jnp.float32)
        r = lax.broadcasted_iota(jnp.int32, (rows, 256), 1).astype(jnp.float32)
        across = (j + 0.5) * (1.0 / 1024.0) - 0.5
        turns = (shifts[level] * across) * ((r + 256.0) * (1.0 / 256.0))
        turns = turns - jnp.round(turns)
        square = turns * turns
        cos = poly(COS, square) * math.sqrt(0.5)
        sin = poly(SIN, square) * turns * math.sqrt(0.5)
        for n in range(stack):
            ph_c[at + n * rows : at + (n + 1) * rows, :] = cos
            ph_s[at + n * rows : at + (n + 1) * rows, :] = sin
        bases.append(at)
        at += rows * stack

    meet(2)
    zsend_one(2, 0)
    zsend_one(2, 1)

    for level, pm in enumerate((p0, p1, p2, p3, p4)):
        rows, stack, wide = OUT[level], STACK[level], WIN[level]
        mp = -(-rows * stack // 128) * 128
        kp = -(-wide * stack // 128) * 128
        tp = taps[level, h[level]]
        wt = weights[level, h[level]]
        if level < LEVELS - 1:
            first = h[level + 1] * HALF + starts[level + 1]
            lane = lax.broadcasted_iota(jnp.int32, (4, 512), 1)
            tp_all = jnp.full((4, 512), -1, jnp.int32)
            wt_all = jnp.zeros((4, 512), jnp.float32)
            for n in range(stack):
                turn = (512 + n * rows - first) % 512
                here = (lane >= n * rows) & (lane < (n + 1) * rows)
                tp_all = jnp.where(here, pltpu.roll(tp, turn, 1) + (n * wide - starts[level]), tp_all)
                wt_all = jnp.where(here, pltpu.roll(wt, turn, 1), wt_all)
            tp, wt = tp_all, wt_all
        ids = lax.broadcasted_iota(jnp.int32, (kp, mp), 0)
        total = jnp.zeros((kp, mp), jnp.float32)
        for s in range(4):
            total = total + jnp.where(tp[s : s + 1, :mp] == ids, wt[s : s + 1, :mp], 0.0)
        pm[...] = total.T[: rows * stack, : wide * stack].astype(jnp.bfloat16)

    pl.when((zl % 2 == 1) & (zh == 0))(lambda: pl.delay(1500))
    pl.when((zl % 2 == 1) & (zh == 1))(lambda: pl.delay(500))
    pl.when((zl % 2 == 1) & (zh == 2))(lambda: pl.delay(4000))
    pl.when((zl % 2 == 1) & (zh == 3))(lambda: pl.delay(2500))
    zsend_one(1, 2)
    zsend_one(2, 2)
    pl.delay(2500)
    pl.when(zl % 2 == 1)(lambda: pl.delay(2500))
    zsend_one(0, 3)
    zsend_one(1, 3)
    zsend_one(2, 3)

    def rotate(prod, level):
        base, rows = bases[level], OUT[level] * STACK[level]
        cos = ph_c[base : base + rows, :]
        sin = ph_s[base : base + rows, :]
        first, second = prod[:, 0:512], prod[:, 512:1024]
        add = first + second
        sub = first - second
        re = cos * add[:, :256] - sin * sub[:, 256:]
        im = cos * add[:, 256:] + sin * sub[:, :256]
        return re, im

    def dot(a, b):
        return jnp.dot(a, b, preferred_element_type=jnp.float32)

    def block_copy(k, o):
        dev, w = near(o)
        return pltpu.make_async_remote_copy(
            src_ref=sbuf.at[k, w],
            dst_ref=rbuf.at[k, my_slot],
            send_sem=ssend.at[k],
            recv_sem=srecv.at[k],
            device_id=dev,
            device_id_type=MESH,
        )

    def all_of(k):
        return pltpu.make_async_remote_copy(
            src_ref=sbuf.at[k, pl.ds(0, 31)],
            dst_ref=rbuf.at[k, pl.ds(0, 31)],
            send_sem=ssend.at[k],
            recv_sem=srecv.at[k],
            device_id=near(others[0])[0],
            device_id_type=MESH,
        )

    def send(k):
        own[2 + k].wait()
        for i in range(1, 4):
            came = (zh + i) % 4
            pltpu.make_async_remote_copy(
                src_ref=zbuf.at[k, came],
                dst_ref=zbuf.at[k, came],
                send_sem=zsend.at[k, 0],
                recv_sem=zrecv.at[k, came],
                device_id=column(came, c),
                device_id_type=MESH,
            ).wait_recv()
        for t in range(2):
            part = zbuf[k, :, :, :, t * 512 : (t + 1) * 512]
            real, imag = part[:, 0], part[:, 1]
            plain = jnp.stack([real, imag], axis=1).reshape(64, 512)
            turned = jnp.stack([imag, -real], axis=1).reshape(64, 512)
            rawk[t * 64 : (t + 1) * 64, 0:512] = plain
            rawk[t * 64 : (t + 1) * 64, 512:1024] = turned
        prod = lax.dot_general(
            beam[...], rawk[...], (((1,), (1,)), ((), ())), preferred_element_type=jnp.float32
        )
        prod = (prod * (1.0 / math.sqrt(512.0))).astype(jnp.bfloat16)
        sbuf[k] = prod.reshape(32, WIN[0], 128)

        for other in others:
            block_copy(k, other).start()
        rbuf[k, my_slot] = sbuf[k, mine]

    def take(k):
        all_of(k).wait_recv()
        came = [rbuf[k, s * 4 : s * 4 + 4].reshape(4 * WIN[0], 128) for s in range(8)]
        lhs = jnp.concatenate(
            [
                jnp.concatenate([piece[:, t * 64 : t * 64 + 64] for piece in came], axis=1)
                for t in range(2)
            ],
            axis=0,
        )
        sub0 = dot(lhs, rtab[...]).astype(jnp.bfloat16)
        sub0 = jnp.concatenate([sub0[: 4 * WIN[0]], sub0[4 * WIN[0] :]], axis=1)
        re, im = rotate(dot(p0[...], sub0), 0)
        half = k % 2 * 512
        x1[k // 2, :, half : half + 256] = re.astype(jnp.bfloat16)
        x1[k // 2, :, half + 256 : half + 512] = im.astype(jnp.bfloat16)
        if k % 2 == 1:
            m = k // 2
            re, im = rotate(dot(p1[...], x1[m]), 1)
            for yh in range(2):
                x2[yh, :, m * 512 : m * 512 + 256] = re[yh * 144 : yh * 144 + 144].astype(jnp.bfloat16)
                x2[yh, :, m * 512 + 256 : m * 512 + 512] = im[yh * 144 : yh * 144 + 144].astype(jnp.bfloat16)

    @pl.when(c == 0)
    def _():
        pl.semaphore_wait(xyready, 1)

    own[0].wait()
    own[1].wait()
    send(0)
    for k in range(1, CHUNKS):
        send(k)
        take(k - 1)
    take(CHUNKS - 1)
    for yh in range(2):
        re, im = rotate(dot(p2[...], x2[yh]), 2)
        for yb in range(2):
            x3[yh, :, yb * 512 : yb * 512 + 256] = re[yb * 144 : yb * 144 + 144].astype(jnp.bfloat16)
            x3[yh, :, yb * 512 + 256 : yb * 512 + 512] = im[yb * 144 : yb * 144 + 144].astype(jnp.bfloat16)
    for yh in range(2):
        re, im = rotate(dot(p3[...], x3[yh]), 3)
        x4[:, yh * 512 : yh * 512 + 256] = re.astype(jnp.bfloat16)
        x4[:, yh * 512 + 256 : yh * 512 + 512] = im.astype(jnp.bfloat16)
    re, im = rotate(dot(p4[...], x4[...]), 4)
    out[0] = re.astype(jnp.bfloat16)
    out[1] = im.astype(jnp.bfloat16)

    for p in range(3):
        for k in range(CHUNKS):
            zcopy(p, k).wait_send()
    for k in range(CHUNKS):
        all_of(k).wait_send()


def on_device(raw, taps, weights, shifts):
    beam, rtab = tables()
    rows = sum(o * s for o, s in zip(OUT, STACK))
    hbm = pl.BlockSpec(memory_space=pltpu.HBM)
    vmem = pl.BlockSpec(memory_space=pltpu.VMEM)
    bf = jnp.bfloat16
    return pl.pallas_call(
        kernel,
        name="backproject",
        out_shape=jax.ShapeDtypeStruct((2, ANGLES, NF), bf),
        in_specs=[hbm] * 6,
        out_specs=vmem,
        scratch_shapes=[
            pltpu.VMEM((LEVELS, 2, 4, 512), jnp.int32),
            pltpu.VMEM((LEVELS, 2, 4, 512), jnp.float32),
            pltpu.SMEM((LEVELS,), jnp.float32),
            pltpu.VMEM((CHUNKS, 4, 2, 8, 1024), bf),
            pltpu.VMEM((768, 1024), bf),
            pltpu.VMEM((512, 512), bf),
            pltpu.VMEM((128, 1024), bf),
            pltpu.VMEM((CHUNKS, 32, WIN[0], 128), bf),
            pltpu.VMEM((CHUNKS, 32, WIN[0], 128), bf),
            pltpu.VMEM((rows, 256), jnp.float32),
            pltpu.VMEM((rows, 256), jnp.float32),
        ]
        + [pltpu.VMEM((OUT[i] * STACK[i], WIN[i] * STACK[i]), bf) for i in range(LEVELS)]
        + [
            pltpu.VMEM((2, 160, 1024), bf),
            pltpu.VMEM((2, 144, 1024), bf),
            pltpu.VMEM((2, 144, 1024), bf),
            pltpu.VMEM((256, 1024), bf),
            pltpu.SemaphoreType.DMA((CHUNKS, 4)),
            pltpu.SemaphoreType.DMA((CHUNKS, 4)),
            pltpu.SemaphoreType.DMA((CHUNKS,)),
            pltpu.SemaphoreType.DMA((CHUNKS,)),
            pltpu.SemaphoreType.DMA((9,)),
            pltpu.SemaphoreType.REGULAR((4,)),
            pltpu.SemaphoreType.REGULAR,
        ],
        compiler_params=pltpu.CompilerParams(
            collective_id=0, has_side_effects=True, vmem_limit_bytes=32 << 20
        ),
    )(*(pltpu.with_memory_space_constraint(a, pltpu.HBM) for a in (raw, taps, weights, shifts, beam, rtab)))


def solution(mesh):
    return jax.shard_map(
        on_device,
        mesh=mesh,
        in_specs=(P(None, "band", "grp"), P(), P(), P()),
        out_specs=P(None, ("grp", "band"), None),
        check_vma=False,
    )
```

```python
import functools
import math

import jax
import jax.numpy as jnp
import numpy as np
from jax import lax
from jax.experimental import pallas as pl
from jax.experimental.pallas import tpu as pltpu
from jax.sharding import PartitionSpec as P

MESH = pl.DeviceIdType.MESH
NF = 256
ANGLES = 512
HALF = 256
LEVELS = 5
WIN = (24, 40, 72, 144, 256)
OUT = (40, 72, 144, 256, 512)
STACK = (4, 4, 2, 1, 1)
CHUNKS = 4


def chain(h, lesser, greater):
    low, starts = 0, [0] * LEVELS
    for level in range(LEVELS - 2, -1, -1):
        low = greater((h[level + 1] * HALF + low) // 2 - 1, 0)
        starts[level] = lesser(low, HALF - WIN[level])
    return starts


def beam_rows():
    rows = []
    for w in range(32):
        h = [w >> (4 - i) & 1 for i in range(5)]
        first = h[0] * HALF + chain(h, min, max)[0]
        rows.append(first + np.arange(WIN[0]))
    return np.concatenate(rows)


def tables():
    a = beam_rows()
    q = np.arange(512)
    beam = 2.0 * np.pi * (a[:, None] * q[None, :] % ANGLES) / ANGLES
    beam = np.concatenate([np.cos(beam), np.sin(beam)], axis=1)
    f = np.arange(NF)
    turn = 2.0 * np.pi * (f[:, None] * f[None, :] % NF) / NF
    cos = jnp.asarray(np.cos(turn), jnp.bfloat16)
    sin = jnp.asarray(np.sin(turn), jnp.bfloat16)
    real = jnp.concatenate([cos, -sin], axis=1)
    imag = jnp.concatenate([sin, cos], axis=1)
    both = jnp.stack([real.reshape(4, 8, 8, 512), imag.reshape(4, 8, 8, 512)], axis=2)
    both = both.transpose(1, 0, 2, 3, 4).reshape(512, 512)
    return jnp.asarray(beam, jnp.bfloat16), both * jnp.bfloat16(1.0 / 16.0)


COS = np.polynomial.chebyshev.Chebyshev.interpolate(
    lambda s: np.cos(2 * np.pi * np.sqrt(s)), 7, domain=[0.0, 0.25]
).convert(kind=np.polynomial.Polynomial).coef
SIN = np.polynomial.chebyshev.Chebyshev.interpolate(
    lambda s: np.sinc(2 * np.sqrt(s)) * 2 * np.pi, 7, domain=[0.0, 0.25]
).convert(kind=np.polynomial.Polynomial).coef


def poly(coef, s):
    out = jnp.full_like(s, float(coef[-1]))
    for value in coef[-2::-1]:
        out = out * s + float(value)
    return out


def kernel(
    raw, taps_hbm, weights_hbm, shifts_hbm, beam_hbm, range_hbm, out,
    taps, weights, shifts, zbuf, beam, rtab, rawk, sbuf, rbuf, ph_c, ph_s, p0, p1, p2, p3, p4, x1, x2, x3, x4,
    zsend, zrecv, ssend, srecv, local, known, xyready,
):
    grp = lax.axis_index("grp")
    band = lax.axis_index("band")
    zh, x, c = band // 8, (band // 2) % 4, band % 2
    zl, y = grp // 4, grp % 4
    h = [c, x % 2, x // 2, y % 2, y // 2]
    mine = h[0] * 16 + h[1] * 8 + h[2] * 4 + h[3] * 2 + h[4]
    starts = chain(h, jnp.minimum, jnp.maximum)
    my_slot = (x * 2 + c) * 4 + y

    bands = [[zh * 8 + (x + dx) % 4 * 2 + co for co in range(2)] for dx in range(4)]
    grps = [zl * 4 + (y + dy) % 4 for dy in range(4)]
    w_x = [(x + dx) % 2 * 8 + (x + dx) % 4 // 2 * 4 for dx in range(4)]
    w_y = [(y + dy) % 2 * 2 + (y + dy) % 4 // 2 for dy in range(4)]
    places = sorted(
        ((dx, dy) for dx in range(4) for dy in range(4)),
        key=lambda o: -min(o[0], 4 - o[0]) - min(o[1], 4 - o[1]),
    )

    def near(other):
        dx, co, dy = other
        return {"band": bands[dx][co], "grp": grps[dy]}, co * 16 + w_x[dx] + w_y[dy]

    own = []
    own.append(pltpu.make_async_copy(beam_hbm, beam, local.at[0]))
    own.append(pltpu.make_async_copy(range_hbm, rtab, local.at[1]))
    for k in range(CHUNKS):
        own.append(
            pltpu.make_async_copy(
                raw.at[:, :, pl.ds(pl.multiple_of(zh * 4096 + k * 1024, 1024), 1024)],
                zbuf.at[k, zh],
                local.at[2 + k],
            )
        )
    small = [
        pltpu.make_async_copy(shifts_hbm, shifts, local.at[6]),
        pltpu.make_async_copy(taps_hbm, taps, local.at[7]),
        pltpu.make_async_copy(weights_hbm, weights, local.at[8]),
    ]
    barrier = pltpu.get_barrier_semaphore()

    def by_zh(values):
        picked = values[0]
        for i in range(1, 4):
            picked = jnp.where(zh == i, values[i], picked)
        return picked

    def signal(sem, to):
        pl.semaphore_signal(sem, inc=1, device_id=to, device_id_type=MESH)

    def column(zo, co):
        return {"band": zo * 8 + x * 2 + co, "grp": grp}

    partner = column(zh, 1 - c)
    soon = ((1, 0), (3, 0), (2, 0), (2, 1))
    late = ((3, 1), (2, 3))
    for pairs, core in ((soon, 0), (late, 1)):
        for hears, speaks in pairs:

            @pl.when(zh == speaks)
            def _(hears=hears, core=core):
                signal(barrier, column(hears, core))

    signal(barrier, partner)

    def greet(o, carry):
        signal(barrier, {"band": zh * 8 + (x + o % 4) % 4 * 2 + 1, "grp": zl * 4 + (y + o // 4) % 4})
        return carry

    lax.fori_loop(1, 16, greet, 0)

    for cp in small + own:
        cp.start()

    def tell(pairs):
        for hears, speaks in pairs:

            @pl.when(zh == hears)
            def _(hears=hears, speaks=speaks):
                pl.semaphore_signal(known.at[speaks], inc=1)
                signal(known.at[speaks], partner)
                for co in range(2):
                    signal(known.at[hears], column(speaks, co))

    @pl.when(c == 0)
    def _():
        pl.semaphore_wait(barrier, by_zh((1, 3, 5, 3)))
        tell(soon)

    def hear_rest():
        pl.semaphore_wait(barrier, by_zh((31, 31, 33, 33)))
        tell(late)
        signal(xyready, partner)

    order = ((1, 3, 2), (0, 2, 3), (0, 1, 3), (0, 1, 2))

    dests = [by_zh([o[p] for o in order]) for p in range(3)]

    def meet(p):
        pl.semaphore_wait(known.at[dests[p]], 1)

    def zcopy(p, k):
        return pltpu.make_async_remote_copy(
            src_ref=raw.at[:, :, pl.ds(pl.multiple_of(dests[p] * 4096 + k * 1024, 1024), 1024)],
            dst_ref=zbuf.at[k, zh],
            send_sem=zsend.at[k, p],
            recv_sem=zrecv.at[k, zh],
            device_id=column(dests[p], c),
            device_id_type=MESH,
        )

    def zsend_one(p, k):
        zcopy(p, k).start()

    meet(0)
    zsend_one(0, 0)
    zsend_one(0, 1)
    zsend_one(0, 2)
    pl.when((c == 1) & (zh != 2))(hear_rest)
    meet(1)
    zsend_one(1, 0)
    zsend_one(1, 1)
    pl.when((c == 1) & (zh == 2))(hear_rest)
    for cp in small:
        cp.wait()

    at = 0
    bases = []
    for level in range(LEVELS):
        rows, stack = OUT[level], STACK[level]
        if level < LEVELS - 1:
            first = h[level + 1] * HALF + starts[level + 1]
        else:
            first = 0
        j = (lax.broadcasted_iota(jnp.int32, (rows, 256), 0) + (h[level] * 512 + first)).astype(jnp.float32)
        r = lax.broadcasted_iota(jnp.int32, (rows, 256), 1).astype(jnp.float32)
        across = (j + 0.5) * (1.0 / 1024.0) - 0.5
        turns = (shifts[level] * across) * ((r + 256.0) * (1.0 / 256.0))
        turns = turns - jnp.round(turns)
        square = turns * turns
        cos = poly(COS, square) * math.sqrt(0.5)
        sin = poly(SIN, square) * turns * math.sqrt(0.5)
        for n in range(stack):
            ph_c[at + n * rows : at + (n + 1) * rows, :] = cos
            ph_s[at + n * rows : at + (n + 1) * rows, :] = sin
        bases.append(at)
        at += rows * stack

    meet(2)
    zsend_one(2, 0)
    zsend_one(2, 1)

    for level, pm in enumerate((p0, p1, p2, p3, p4)):
        rows, stack, wide = OUT[level], STACK[level], WIN[level]
        mp = -(-rows * stack // 128) * 128
        kp = -(-wide * stack // 128) * 128
        tp = taps[level, h[level]]
        wt = weights[level, h[level]]
        if level < LEVELS - 1:
            first = h[level + 1] * HALF + starts[level + 1]
            lane = lax.broadcasted_iota(jnp.int32, (4, 512), 1)
            tp_all = jnp.full((4, 512), -1, jnp.int32)
            wt_all = jnp.zeros((4, 512), jnp.float32)
            for n in range(stack):
                turn = (512 + n * rows - first) % 512
                here = (lane >= n * rows) & (lane < (n + 1) * rows)
                tp_all = jnp.where(here, pltpu.roll(tp, turn, 1) + (n * wide - starts[level]), tp_all)
                wt_all = jnp.where(here, pltpu.roll(wt, turn, 1), wt_all)
            tp, wt = tp_all, wt_all
        ids = lax.broadcasted_iota(jnp.int32, (kp, mp), 0)
        total = jnp.zeros((kp, mp), jnp.float32)
        for s in range(4):
            total = total + jnp.where(tp[s : s + 1, :mp] == ids, wt[s : s + 1, :mp], 0.0)
        pm[...] = total.T[: rows * stack, : wide * stack].astype(jnp.bfloat16)

    pl.when((zl % 2 == 1) & (zh == 0))(lambda: pl.delay(1500))
    pl.when((zl % 2 == 1) & (zh == 1))(lambda: pl.delay(500))
    pl.when((zl % 2 == 1) & (zh == 2))(lambda: pl.delay(4000))
    pl.when((zl % 2 == 1) & (zh == 3))(lambda: pl.delay(2500))
    zsend_one(1, 2)
    zsend_one(2, 2)
    pl.delay(2500)
    pl.when(zl % 2 == 1)(lambda: pl.delay(2500))
    zsend_one(0, 3)
    zsend_one(1, 3)
    zsend_one(2, 3)

    def rotate(prod, level):
        base, rows = bases[level], OUT[level] * STACK[level]
        cos = ph_c[base : base + rows, :]
        sin = ph_s[base : base + rows, :]
        first, second = prod[:, 0:512], prod[:, 512:1024]
        add = first + second
        sub = first - second
        re = cos * add[:, :256] - sin * sub[:, 256:]
        im = cos * add[:, 256:] + sin * sub[:, :256]
        return re, im

    def dot(a, b):
        return jnp.dot(a, b, preferred_element_type=jnp.float32)

    def block_copy(k, o):
        dev, w = near(o)
        return pltpu.make_async_remote_copy(
            src_ref=sbuf.at[k, w],
            dst_ref=rbuf.at[k, my_slot],
            send_sem=ssend.at[k],
            recv_sem=srecv.at[k],
            device_id=dev,
            device_id_type=MESH,
        )

    def all_of(k):
        return pltpu.make_async_remote_copy(
            src_ref=sbuf.at[k, pl.ds(0, 31)],
            dst_ref=rbuf.at[k, pl.ds(0, 31)],
            send_sem=ssend.at[k],
            recv_sem=srecv.at[k],
            device_id=near((1, 0, 0))[0],
            device_id_type=MESH,
        )

    def send(k):
        own[2 + k].wait()
        for i in range(1, 4):
            came = (zh + i) % 4
            pltpu.make_async_remote_copy(
                src_ref=zbuf.at[k, came],
                dst_ref=zbuf.at[k, came],
                send_sem=zsend.at[k, 0],
                recv_sem=zrecv.at[k, came],
                device_id=column(came, c),
                device_id_type=MESH,
            ).wait_recv()
        for t in range(2):
            part = zbuf[k, :, :, :, t * 512 : (t + 1) * 512]
            real, imag = part[:, 0], part[:, 1]
            plain = jnp.stack([real, imag], axis=1).reshape(64, 512)
            turned = jnp.stack([imag, -real], axis=1).reshape(64, 512)
            rawk[t * 64 : (t + 1) * 64, 0:512] = plain
            rawk[t * 64 : (t + 1) * 64, 512:1024] = turned
        for core in range(2):
            prod = lax.dot_general(
                beam[core * 384 : core * 384 + 384],
                rawk[...],
                (((1,), (1,)), ((), ())),
                preferred_element_type=jnp.float32,
            )
            prod = (prod * (1.0 / math.sqrt(512.0))).astype(jnp.bfloat16)
            sbuf[k, core * 16 : core * 16 + 16] = prod.reshape(16, WIN[0], 128)
            for dx, dy in places:
                if dx or dy:
                    block_copy(k, (dx, core, dy)).start()
                else:
                    pl.when(c != core)(block_copy(k, (dx, core, dy)).start)
        rbuf[k, my_slot] = sbuf[k, mine]

    def take(k):
        all_of(k).wait_recv()
        came = [rbuf[k, s * 4 : s * 4 + 4].reshape(4 * WIN[0], 128) for s in range(8)]
        lhs = jnp.concatenate(
            [
                jnp.concatenate([piece[:, t * 64 : t * 64 + 64] for piece in came], axis=1)
                for t in range(2)
            ],
            axis=0,
        )
        sub0 = dot(lhs, rtab[...]).astype(jnp.bfloat16)
        sub0 = jnp.concatenate([sub0[: 4 * WIN[0]], sub0[4 * WIN[0] :]], axis=1)
        re, im = rotate(dot(p0[...], sub0), 0)
        half = k % 2 * 512
        x1[k // 2, :, half : half + 256] = re.astype(jnp.bfloat16)
        x1[k // 2, :, half + 256 : half + 512] = im.astype(jnp.bfloat16)
        if k % 2 == 1:
            m = k // 2
            re, im = rotate(dot(p1[...], x1[m]), 1)
            for yh in range(2):
                x2[yh, :, m * 512 : m * 512 + 256] = re[yh * 144 : yh * 144 + 144].astype(jnp.bfloat16)
                x2[yh, :, m * 512 + 256 : m * 512 + 512] = im[yh * 144 : yh * 144 + 144].astype(jnp.bfloat16)

    @pl.when(c == 0)
    def _():
        pl.semaphore_wait(xyready, 1)

    own[0].wait()
    own[1].wait()
    send(0)
    for k in range(1, CHUNKS):
        send(k)
        take(k - 1)
    take(CHUNKS - 1)
    for yh in range(2):
        re, im = rotate(dot(p2[...], x2[yh]), 2)
        for yb in range(2):
            x3[yh, :, yb * 512 : yb * 512 + 256] = re[yb * 144 : yb * 144 + 144].astype(jnp.bfloat16)
            x3[yh, :, yb * 512 + 256 : yb * 512 + 512] = im[yb * 144 : yb * 144 + 144].astype(jnp.bfloat16)
    for yh in range(2):
        re, im = rotate(dot(p3[...], x3[yh]), 3)
        x4[:, yh * 512 : yh * 512 + 256] = re.astype(jnp.bfloat16)
        x4[:, yh * 512 + 256 : yh * 512 + 512] = im.astype(jnp.bfloat16)
    re, im = rotate(dot(p4[...], x4[...]), 4)
    out[0] = re.astype(jnp.bfloat16)
    out[1] = im.astype(jnp.bfloat16)

    for p in range(3):
        for k in range(CHUNKS):
            zcopy(p, k).wait_send()
    for k in range(CHUNKS):
        all_of(k).wait_send()


def on_device(raw, taps, weights, shifts):
    beam, rtab = tables()
    rows = sum(o * s for o, s in zip(OUT, STACK))
    hbm = pl.BlockSpec(memory_space=pltpu.HBM)
    vmem = pl.BlockSpec(memory_space=pltpu.VMEM)
    bf = jnp.bfloat16
    return pl.pallas_call(
        kernel,
        name="backproject",
        out_shape=jax.ShapeDtypeStruct((2, ANGLES, NF), bf),
        in_specs=[hbm] * 6,
        out_specs=vmem,
        scratch_shapes=[
            pltpu.VMEM((LEVELS, 2, 4, 512), jnp.int32),
            pltpu.VMEM((LEVELS, 2, 4, 512), jnp.float32),
            pltpu.SMEM((LEVELS,), jnp.float32),
            pltpu.VMEM((CHUNKS, 4, 2, 8, 1024), bf),
            pltpu.VMEM((768, 1024), bf),
            pltpu.VMEM((512, 512), bf),
            pltpu.VMEM((128, 1024), bf),
            pltpu.VMEM((CHUNKS, 32, WIN[0], 128), bf),
            pltpu.VMEM((CHUNKS, 32, WIN[0], 128), bf),
            pltpu.VMEM((rows, 256), jnp.float32),
            pltpu.VMEM((rows, 256), jnp.float32),
        ]
        + [pltpu.VMEM((OUT[i] * STACK[i], WIN[i] * STACK[i]), bf) for i in range(LEVELS)]
        + [
            pltpu.VMEM((2, 160, 1024), bf),
            pltpu.VMEM((2, 144, 1024), bf),
            pltpu.VMEM((2, 144, 1024), bf),
            pltpu.VMEM((256, 1024), bf),
            pltpu.SemaphoreType.DMA((CHUNKS, 4)),
            pltpu.SemaphoreType.DMA((CHUNKS, 4)),
            pltpu.SemaphoreType.DMA((CHUNKS,)),
            pltpu.SemaphoreType.DMA((CHUNKS,)),
            pltpu.SemaphoreType.DMA((9,)),
            pltpu.SemaphoreType.REGULAR((4,)),
            pltpu.SemaphoreType.REGULAR,
        ],
        compiler_params=pltpu.CompilerParams(
            collective_id=0, has_side_effects=True, vmem_limit_bytes=32 << 20
        ),
    )(*(pltpu.with_memory_space_constraint(a, pltpu.HBM) for a in (raw, taps, weights, shifts, beam, rtab)))


def solution(mesh):
    return jax.shard_map(
        on_device,
        mesh=mesh,
        in_specs=(P(None, "band", "grp"), P(), P(), P()),
        out_specs=P(None, ("grp", "band"), None),
        check_vma=False,
    )
```
